512 devices in a mesh: pop: 32 (over z, x_lo, core), mp: 16 (over x_hi, y).
Axes of the slice: x: 4 (x_hi: 2, x_lo: 2; x = x_hi * 2 + x_lo), y: 8, z: 8, core: 2. Of those that a mesh axis runs over, the one named last changes fastest.
Arguments:
- prompts: bfloat16 [128, 128, 4096], P('pop'), may hold values from -9 to 9
- gate_weight: bfloat16 [4096, 8192], P('pop', 'mp'), may hold values from -0.09375 to 0.09375
- up_weight: bfloat16 [4096, 8192], P('pop', 'mp'), may hold values from -0.09375 to 0.09375
- reward_head: bfloat16 [8192], P('mp'), may hold values from -0.0625 to 0.0625
- member_seeds: int32 [128], P('pop'), may hold values from 0 to 1073741823
- counters: int32 [128], P('pop'), may hold values from 0 to 65535
- member_ranks: int32 [128], P('pop'), may hold values from 0 to 127, each once
Outputs:
- new_gate: bfloat16 [4096, 8192], P('pop', 'mp')
- new_up: bfloat16 [4096, 8192], P('pop', 'mp')
- scores: float32 [128], P('pop')
The draws below stay inside these ranges and needn't reach their ends.
All inputs are finite; a program needn't handle non-finite values.
Results may differ from the reference program's by a relative error of at most 0.014.
Values may be sent and summed in bfloat16 or wider, within the bound.
A program may use at most 64 MiB of HBM per device.

```python
import jax
import jax.numpy as jnp
from jax import lax

D = 4096
HID = 8192
SEQ = 128
MEMBERS = 128


def draw_prompts(key, part):
    member_pos = jnp.arange(MEMBERS, dtype=jnp.float32) / max(MEMBERS - 1, 1)
    sample = jnp.clip(jax.random.normal(key, (MEMBERS, SEQ, D), jnp.float32), -6.0, 6.0)
    scaling = 0.5 + member_pos
    return (sample * scaling[:, None, None]).astype(jnp.bfloat16)


def plant(result, key, low, high):
    longest = result.shape.index(max(result.shape))
    spots = []
    for shift in (0, 1):
        where = [jax.random.randint(jax.random.fold_in(key, axis), (), 0, length) for axis, length in enumerate(result.shape)]
        where[longest] = (where[longest] + shift) % result.shape[longest]
        spots.append(tuple(where))
    return result.at[spots[0]].set(low).at[spots[1]].set(high)


def block_scale(own_key, extent, pieces, smallest, largest):
    factor_of, own = 1.0, jax.random.fold_in(own_key, 6)
    for axis_at, blocks in pieces:
        steps = jnp.exp(jax.random.uniform(jax.random.fold_in(own, axis_at), (blocks,), jnp.float32, smallest / len(pieces), largest / len(pieces)))
        factor_of = factor_of * jnp.repeat(steps, extent[axis_at] // blocks).reshape([-1 if axis == axis_at else 1 for axis in range(len(extent))])
    return factor_of


def bell_draw(rng, extent, width, most, pieces=(), kind=jnp.bfloat16):
    result = width * jax.random.normal(rng, extent, jnp.float32)
    if pieces:
        result = result * block_scale(rng, extent, pieces, -0.22, 0.18)
    return jnp.clip(result, -most, most).astype(kind)


def setup_inputs(seed: int = 0) -> dict:
    keys = jax.random.split(jax.random.key(seed), 8)
    prompts = draw_prompts(jax.random.fold_in(keys[7], 71), 0)
    gate_weight = bell_draw(keys[1], (D, HID), D ** -0.5, 0.09375, ((0, 32), (1, 16)))
    up_weight = bell_draw(keys[2], (D, HID), D ** -0.5, 0.09375, ((0, 32), (1, 16)))
    reward_head = bell_draw(keys[3], (HID,), HID ** -0.5, 0.0625, ((0, 16),))
    member_seeds = plant(jax.random.randint(keys[4], (MEMBERS,), 0, 1073741824), jax.random.fold_in(keys[4], 1), 0, 1073741823).astype(jnp.int32)
    counters = plant(jax.random.randint(keys[5], (MEMBERS,), 0, 65536), jax.random.fold_in(keys[5], 1), 0, 65535).astype(jnp.int32)
    member_ranks = jax.random.permutation(keys[6], MEMBERS).astype(jnp.int32)
    return {"prompts": prompts, "gate_weight": gate_weight, "up_weight": up_weight, "reward_head": reward_head, "member_seeds": member_seeds, "counters": counters, "member_ranks": member_ranks}


sigma_perturb = 0.004
learn_rate = 0.0016

def shift_down(number, amount):
    return lax.shift_right_logical(number, jnp.full_like(number, amount))

def mix_bits(number):
    number = number ^ shift_down(number, 16)
    number = number * 2146121005
    number = number ^ shift_down(number, 15)
    number = number * -2073254261
    return number ^ shift_down(number, 16)

def factor_rows(seed_list, counter_list, slot, positions):
    anchor = mix_bits(seed_list * 1103515245 + mix_bits(counter_list * 668265263 + slot * 374761393))
    hashed = mix_bits(anchor[:, None] + positions[None, :] * -1640531535)
    uniform_part = shift_down(hashed, 8).astype(jnp.float32) * (1.0 / 16777216.0)
    return (2.0 * uniform_part - 1.0 + 1.0 / 16777216.0) * 1.7320508075688772

def reference(prompts, gate_weight, up_weight, reward_head, member_seeds, counters, member_ranks):
    fitness = (member_ranks.astype(jnp.float32) + 0.5) / MEMBERS - 0.5
    scaling = learn_rate / (MEMBERS * sigma_perturb)
    row_index = jnp.arange(D, dtype=jnp.int32)
    col_index = jnp.arange(HID, dtype=jnp.int32)

    def updated(weight, slot):
        left_factor = (factor_rows(member_seeds, counters, slot, row_index) * fitness[:, None]).astype(jnp.bfloat16)
        right_factor = factor_rows(member_seeds, counters, slot + 1, col_index).astype(jnp.bfloat16)
        update_term = scaling * jnp.dot(left_factor.T, right_factor, preferred_element_type=jnp.float32)
        return (weight.astype(jnp.float32) + update_term).astype(jnp.bfloat16)
    new_gate = updated(gate_weight, 0)
    new_up = updated(up_weight, 2)
    later = counters + 1

    def member(inputs):
        sample, seed_one, counter_one = inputs
        seed_row = seed_one[None]
        counter_row = counter_one[None]
        gate_vec = factor_rows(seed_row, counter_row, 0, row_index)[0].astype(jnp.bfloat16)
        gate_col = factor_rows(seed_row, counter_row, 1, col_index)[0]
        up_vec = factor_rows(seed_row, counter_row, 2, row_index)[0].astype(jnp.bfloat16)
        up_col = factor_rows(seed_row, counter_row, 3, col_index)[0]
        gate_value = jnp.dot(sample, new_gate, preferred_element_type=jnp.float32) + sigma_perturb * jnp.dot(sample, gate_vec, preferred_element_type=jnp.float32)[:, None] * gate_col[None, :]
        up_value = jnp.dot(sample, new_up, preferred_element_type=jnp.float32) + sigma_perturb * jnp.dot(sample, up_vec, preferred_element_type=jnp.float32)[:, None] * up_col[None, :]
        hidden = (jax.nn.silu(gate_value) * up_value).astype(jnp.bfloat16)
        return jnp.sum(jnp.dot(hidden, reward_head, preferred_element_type=jnp.float32)) / SEQ
    rewards = lax.map(member, (prompts, member_seeds, later))
    reward_mean = jnp.mean(rewards)
    reward_var = jnp.mean((rewards - reward_mean) ** 2)
    scores = (rewards - reward_mean) / jnp.sqrt(reward_var + 1e-05)
    return (new_gate, new_up, scores)
```

```python
import functools

import jax
import jax.numpy as jnp
from jax import lax
from jax.experimental import pallas as pl
from jax.experimental.pallas import tpu as pltpu
from jax.sharding import PartitionSpec as P

MESH = pl.DeviceIdType.MESH
SIGMA = 0.004
RATE = 0.0016
ROOT3 = 1.7320508075688772
ZED = 8
GROUP = 16

UP_LINK = [(0, 0, 0), (0, 0, 1), (-1, 0, 0), (0, 1, 1), (-2, 0, 0), (-1, 0, 1), (-3, 0, 0), (-1, 1, 1), (-2, 0, 1), (-2, 1, 1)]
DOWN_LINK = [(-o, w, 1 - h) for o, w, h in UP_LINK]
SIDE_LINK = [(0, 0, 1), (0, 0, 0), (-1, 0, 0), (1, 0, 1), (-2, 0, 0), (2, 0, 1), (-3, 0, 0), (3, 0, 1), (-4, 0, 0), (4, 0, 1)]
SENDS = [UP_LINK, DOWN_LINK, SIDE_LINK]
ARRIVALS = [
    [(o - 1, w, h) for o, w, h in UP_LINK],
    [(o + 1, w, h) for o, w, h in DOWN_LINK],
    [(o, 1 - w, h) for o, w, h in SIDE_LINK],
]
STEPS = len(UP_LINK)


def same_piece(a, b):
    return (a[0] - b[0]) % ZED == 0 and a[1:] == b[1:]


def right_shift(v, amount):
    return lax.shift_right_logical(v, jnp.full_like(v, amount))


def mix(v):
    v = v ^ right_shift(v, 16)
    v = v * 2146121005
    v = v ^ right_shift(v, 15)
    v = v * -2073254261
    return v ^ right_shift(v, 16)


def anchor_of(seed, counter, slot):
    return mix(seed * 1103515245 + mix(counter * 668265263 + slot * 374761393))


def stream(anchor, position):
    h = mix(anchor + position * -1640531535)
    odd = (right_shift(h, 7) | 1) - 16777216
    return odd.astype(jnp.float32) * (ROOT3 / 16777216.0)


def kernel(
    mp_size, seeds, counters, ranks, prompts, gate_w, up_w, head,
    new_gate, new_up, scores,
    xall, wbuf, acc, lbuf, rbuf, vbuf, cbuf, ubuf, wown,
    s_own, s_sib, s_chip, s_all, r_own, r_sib, r_part, r_all, t_part, t_all,
    ring_s, ring_r, one_s, one_r, seed_s, seed_r, red_s, red_r, local_sem,
):
    rows, cols = gate_w.shape
    half = cols // 2
    tokens, width = prompts.shape
    members_here = seeds.shape[0]
    p = lax.axis_index("pop")
    m = lax.axis_index("mp")
    z = p // 4
    xl = lax.rem(p // 2, 2)
    c = lax.rem(p, 2)
    q = p // 2
    members_all = 128

    def pop_of(zz, xx, cc):
        return (zz * 2 + xx) * 2 + cc

    sibling = (pop_of(z, xl, 1 - c), m)
    up = (pop_of(lax.rem(z + 1, ZED), xl, c), m)
    down = (pop_of(lax.rem(z + ZED - 1, ZED), xl, c), m)
    side = (pop_of(z, 1 - xl, c), m)
    links = [up, down, side]

    def chip_peer(i):
        return (2 * lax.rem(q + i, GROUP) + c, m)

    def mp_peer(i):
        return (p, lax.rem(m + i, mp_size))

    barrier = pltpu.get_barrier_semaphore()
    pl.semaphore_signal(barrier, inc=1, device_id=sibling, device_id_type=MESH)

    def greet(i, carry):
        pl.semaphore_signal(barrier, inc=1, device_id=chip_peer(i), device_id_type=MESH)
        return carry

    def greet_mp(i, carry):
        pl.semaphore_signal(barrier, inc=1, device_id=mp_peer(i), device_id_type=MESH)
        return carry

    lax.fori_loop(1, GROUP, greet, 0)
    lax.fori_loop(1, mp_size, greet_mp, 0)

    my_cols = pl.ds(pl.multiple_of(c * half, half), half)
    sib_cols = pl.ds(pl.multiple_of((1 - c) * half, half), half)
    own_rows = pl.ds(pl.multiple_of(c * tokens, tokens), tokens)
    keep_gate = pltpu.make_async_copy(gate_w.at[:, my_cols], wbuf.at[p, :, pl.ds(0, half)], local_sem.at[0])
    keep_up = pltpu.make_async_copy(up_w.at[:, my_cols], wbuf.at[p, :, pl.ds(half, half)], local_sem.at[1])
    keep_gate.start()
    keep_up.start()
    own_prompts = pltpu.make_async_copy(prompts, xall.at[own_rows], local_sem.at[2])
    own_prompts.start()
    load_gate = pltpu.make_async_copy(gate_w, wown.at[0], local_sem.at[3])
    load_up = pltpu.make_async_copy(up_w, wown.at[1], local_sem.at[4])
    load_gate.start()
    load_up.start()

    lane = lax.broadcasted_iota(jnp.int32, (8, 128), 1)
    sub = lax.broadcasted_iota(jnp.int32, (8, 128), 0)
    block = jnp.zeros((8, 128), jnp.int32)
    for i in range(members_here):
        here = lane == p * members_here + i
        for row, values in enumerate((seeds, counters, ranks)):
            block = jnp.where(here & (sub == row), values[i], block)
    s_own[...] = block

    pl.semaphore_wait(barrier, GROUP + mp_size - 1)

    def remote(src, dst, send, recv, device):
        return pltpu.make_async_remote_copy(
            src_ref=src, dst_ref=dst, send_sem=send, recv_sem=recv, device_id=device, device_id_type=MESH
        )

    give_gate = remote(gate_w.at[:, sib_cols], wbuf.at[p, :, pl.ds(0, half)], one_s.at[0], one_r.at[0], sibling)
    give_up = remote(up_w.at[:, sib_cols], wbuf.at[p, :, pl.ds(half, half)], one_s.at[1], one_r.at[1], sibling)
    give_seeds = remote(s_own, s_sib, one_s.at[2], one_r.at[2], sibling)
    give_prompts = remote(prompts, xall.at[own_rows], one_s.at[3], one_r.at[3], sibling)
    give_gate.start()
    give_up.start()
    give_seeds.start()

    def ring_copy(link, index):
        offset, other, core = SENDS[link][index]
        column = 1 - xl if other else xl
        where = pop_of(lax.rem(z + offset + 2 * ZED, ZED), column, core)
        piece = wbuf.at[where]
        return remote(piece, piece, ring_s.at[link, index], ring_r.at[link, index], links[link])

    def pass_on(piece):
        for link in range(3):
            for index, sent in enumerate(SENDS[link]):
                if same_piece(piece, sent):
                    ring_copy(link, index).start()

    def arrive(step):
        for link in range(3):
            ring_copy(link, step).wait_recv()
            pass_on(ARRIVALS[link][step])

    keep_gate.wait()
    keep_up.wait()
    give_gate.wait_recv()
    give_up.wait_recv()
    for index in (0, 1):
        for link in range(3):
            ring_copy(link, index).start()
    give_prompts.start()

    give_seeds.wait_recv()
    s_chip[...] = s_own[...] + s_sib[...]
    s_all[q] = s_chip[...]

    def seed_copy(i):
        return remote(s_chip, s_all.at[q], seed_s.at[i], seed_r.at[i], chip_peer(i))

    def over_peers(act, count=GROUP):
        def step(i, carry):
            act(i)
            return carry

        lax.fori_loop(1, count, step, 0)

    over_peers(lambda i: seed_copy(i).start())

    acc[...] = jnp.zeros_like(acc)
    arrive(0)
    over_peers(lambda i: seed_copy(i).wait_recv())
    table = s_all[0]
    for i in range(1, GROUP):
        table = table + s_all[i]
    seed_row = table[0:1, :]
    count_row = table[1:2, :]
    fit_row = (table[2:3, :].astype(jnp.float32) + 0.5) / members_all - 0.5
    left_gate = anchor_of(seed_row, count_row, 0)
    left_up = anchor_of(seed_row, count_row, 2)
    right_gate = anchor_of(seed_row, count_row, 1)
    right_up = anchor_of(seed_row, count_row, 3)
    scaling = RATE / (members_all * SIGMA)

    def hash_left(first, count):
        def step(i, carry):
            start = pl.multiple_of(i * 128, 128)
            position = start + lax.broadcasted_iota(jnp.int32, (128, 128), 0)
            lbuf[pl.ds(start, 128), 0:128] = (stream(left_gate, position) * fit_row).astype(jnp.bfloat16)
            lbuf[pl.ds(start, 128), 128:256] = (stream(left_up, position) * fit_row).astype(jnp.bfloat16)
            return carry

        lax.fori_loop(first, first + count, step, 0)

    def hash_right():
        def step(i, carry):
            start = pl.multiple_of(i * 128, 128)
            position = m * cols + start + lax.broadcasted_iota(jnp.int32, (128, 128), 0)
            rbuf[pl.ds(start, 128), 0:128] = stream(right_gate, position).astype(jnp.bfloat16)
            rbuf[pl.ds(start, 128), 128:256] = stream(right_up, position).astype(jnp.bfloat16)
            return carry

        lax.fori_loop(0, cols // 128, step, 0)

    def fresh_rows():
        own = pl.ds(pl.multiple_of(p * rows, rows), rows)
        load_gate.wait()
        load_up.wait()
        for index, out in enumerate((new_gate, new_up)):
            part = pl.ds(index * 128, 128)
            delta = lax.dot_general(
                lbuf[own, part], rbuf[:, part], (((1,), (1,)), ((), ())), preferred_element_type=jnp.float32
            )
            out[...] = (wown[index].astype(jnp.float32) + scaling * delta).astype(out.dtype)

    def hash_members():
        pick = lane == q * 8 + sub
        columns = [
            jnp.sum(
                jnp.where(pick, anchor_of(seed_row, count_row + 1, slot), 0), axis=1, keepdims=True
            )
            for slot in range(4)
        ]
        wide = lax.broadcasted_iota(jnp.int32, (8, 1024), 1)
        for start in range(0, width, 1024):
            vbuf[0:8, start : start + 1024] = stream(columns[0], wide + start)
            vbuf[8:16, start : start + 1024] = stream(columns[2], wide + start)
        here = m * cols + c * half + lax.broadcasted_iota(jnp.int32, (8, half), 1)
        cbuf[0:8, :] = stream(columns[1], here) * SIGMA
        cbuf[8:16, :] = stream(columns[3], here) * SIGMA

    tile = 256
    n_tiles = 2 * tokens // tile

    def project():
        def step(i, carry):
            r = pl.ds(pl.multiple_of(i * tile, tile), tile)
            own = lax.dot_general(
                xall[r, :], vbuf[...].astype(jnp.bfloat16), (((1,), (1,)), ((), ())),
                preferred_element_type=jnp.float32,
            )
            ubuf[r, 0:16] = own
            return carry

        lax.fori_loop(0, n_tiles, step, 0)

    def low_rank():
        def step(i, carry):
            r = pl.ds(pl.multiple_of(i * tile, tile), tile)
            zl = jnp.dot(xall[r, :], lbuf[...], preferred_element_type=jnp.float32) * scaling
            zl = zl.astype(jnp.bfloat16)
            for index in range(2):
                part = slice(index * 128, index * 128 + 128)
                acc[r, index * half : (index + 1) * half] += lax.dot_general(
                    zl[:, part],
                    rbuf[pl.ds(pl.multiple_of(c * half, half), half), part],
                    (((1,), (1,)), ((), ())),
                    preferred_element_type=jnp.float32,
                )
            return carry

        lax.fori_loop(0, n_tiles, step, 0)

    seq = 2 * tokens // 8

    def rank_one():
        for i in range(8):
            r = slice(i * seq, (i + 1) * seq)
            for index in range(2):
                s = slice(index * half, (index + 1) * half)
                j = index * 8 + i
                acc[r, s] += ubuf[r, j : j + 1] * cbuf[j : j + 1, :]

    def multiply(offset, other, core=None):
        zz = lax.rem(z + offset + ZED, ZED)
        column = 1 - xl if other else xl
        first = pop_of(zz, column, core or 0)
        depth = rows if core is not None else 2 * rows
        k = pl.ds(pl.multiple_of(first * rows, rows), depth)
        w_of = (lambda: wbuf[first]) if core is not None else (lambda: wbuf[pl.ds(first, 2)].reshape(depth, cols))

        def step(i, carry):
            r = pl.ds(pl.multiple_of(i * tile, tile), tile)
            acc[r, :] += jnp.dot(xall[r, k], w_of(), preferred_element_type=jnp.float32)
            return carry

        lax.fori_loop(0, n_tiles, step, 0)

    hash_left(0, 8)
    arrive(1)
    hash_left(8, 10)
    own_prompts.wait()
    give_prompts.wait_recv()
    arrive(2)
    hash_left(18, 14)
    arrive(3)
    hash_right()
    fresh_rows()
    hash_members()
    arrive(4)
    low_rank()
    arrive(5)
    project()
    rank_one()
    arrive(6)
    multiply(0, 0)
    multiply(0, 1)
    multiply(-1, 0)
    multiply(1, 0)
    arrive(7)
    multiply(-1, 1)
    multiply(1, 1)
    multiply(-2, 0)
    multiply(2, 0)
    multiply(4, 0)
    arrive(8)
    multiply(-2, 1)
    multiply(2, 1)
    multiply(-3, 0)
    multiply(3, 0)
    multiply(-3, 1, 0)
    multiply(3, 1, 1)
    multiply(-4, 1, 0)
    arrive(9)
    multiply(-3, 1, 1)
    multiply(3, 1, 0)
    multiply(4, 1, 1)

    head_row = head[:, my_cols].astype(jnp.float32)
    parts = []
    for i in range(8):
        r = slice(i * seq, (i + 1) * seq)
        gate = acc[r, 0:half]
        value = gate / (1.0 + jnp.exp(-gate)) * acc[r, half:cols]
        parts.append(jnp.sum(value, axis=0, keepdims=True))
    summed = jnp.sum(jnp.concatenate(parts, axis=0) * head_row, axis=1, keepdims=True)
    r_own[...] = jnp.where(lane == q * 8 + sub, summed, 0.0)

    give_reward = remote(r_own, r_sib, one_s.at[4], one_r.at[4], sibling)
    give_reward.start()
    give_reward.wait_recv()
    r_part[...] = r_own[...] + r_sib[...]
    r_all[m] = r_part[...]

    def part_copy(i):
        return remote(r_part, r_all.at[m], red_s.at[0, i], red_r.at[0, i], mp_peer(i))

    over_peers(lambda i: part_copy(i).start(), mp_size)
    over_peers(lambda i: part_copy(i).wait_recv(), mp_size)
    t_part[...] = jnp.sum(r_all[...], axis=0)
    t_all[q] = t_part[...]

    def total_copy(i):
        return remote(t_part, t_all.at[q], red_s.at[1, i], red_r.at[1, i], chip_peer(i))

    over_peers(lambda i: total_copy(i).start())
    over_peers(lambda i: total_copy(i).wait_recv())
    rewards = jnp.sum(jnp.sum(t_all[...], axis=0), axis=0, keepdims=True) / seq
    mean = jnp.sum(rewards, axis=1, keepdims=True) / members_all
    spread = jnp.sum((rewards - mean) ** 2, axis=1, keepdims=True) / members_all
    result = (rewards - mean) / jnp.sqrt(spread + 1e-05)
    for i in range(members_here):
        scores[i] = jnp.sum(jnp.where(lane[0:1] == p * members_here + i, result, 0.0))

    give_gate.wait_send()
    give_up.wait_send()
    give_seeds.wait_send()
    give_prompts.wait_send()
    give_reward.wait_send()
    for link in range(3):
        for index in range(STEPS):
            ring_copy(link, index).wait_send()
    over_peers(lambda i: seed_copy(i).wait_send())
    over_peers(lambda i: part_copy(i).wait_send(), mp_size)
    over_peers(lambda i: total_copy(i).wait_send())


def shards(mp_size, prompts, gate_weight, up_weight, reward_head, member_seeds, counters, member_ranks):
    members_here, seq, width = prompts.shape
    rows, cols = gate_weight.shape
    tokens = members_here * seq
    half = cols // 2
    any_space = pl.BlockSpec(memory_space=pl.ANY)
    vmem = pl.BlockSpec(memory_space=pltpu.VMEM)
    smem = pl.BlockSpec(memory_space=pltpu.SMEM)
    tile_f32 = pltpu.VMEM((8, 128), jnp.float32)
    tile_i32 = pltpu.VMEM((8, 128), jnp.int32)
    dma = pltpu.SemaphoreType.DMA
    return pl.pallas_call(
        functools.partial(kernel, mp_size),
        out_shape=(
            jax.ShapeDtypeStruct((rows, cols), jnp.bfloat16),
            jax.ShapeDtypeStruct((rows, cols), jnp.bfloat16),
            jax.ShapeDtypeStruct((members_here,), jnp.float32),
        ),
        in_specs=[smem, smem, smem, any_space, any_space, any_space, vmem],
        out_specs=(vmem, vmem, smem),
        scratch_shapes=[
            pltpu.VMEM((2 * tokens, width), jnp.bfloat16),
            pltpu.VMEM((2 * GROUP, rows, cols), jnp.bfloat16),
            pltpu.VMEM((2 * tokens, cols), jnp.float32),
            pltpu.VMEM((width, 256), jnp.bfloat16),
            pltpu.VMEM((cols, 256), jnp.bfloat16),
            pltpu.VMEM((16, width), jnp.float32),
            pltpu.VMEM((16, half), jnp.float32),
            pltpu.VMEM((2 * tokens, 128), jnp.float32),
            pltpu.VMEM((2, rows, cols), jnp.bfloat16),
            tile_i32,
            tile_i32,
            tile_i32,
            pltpu.VMEM((GROUP, 8, 128), jnp.int32),
            tile_f32,
            tile_f32,
            tile_f32,
            pltpu.VMEM((mp_size, 8, 128), jnp.float32),
            tile_f32,
            pltpu.VMEM((GROUP, 8, 128), jnp.float32),
            dma((3, STEPS)),
            dma((3, STEPS)),
            dma((5,)),
            dma((5,)),
            dma((GROUP,)),
            dma((GROUP,)),
            dma((2, GROUP)),
            dma((2, GROUP)),
            dma((5,)),
        ],
        compiler_params=pltpu.CompilerParams(
            collective_id=0, has_side_effects=True, vmem_limit_bytes=48 * 1024 * 1024
        ),
        name="generation",
    )(
        member_seeds,
        counters,
        member_ranks,
        prompts.reshape(tokens, width),
        gate_weight,
        up_weight,
        reward_head.reshape(1, cols),
    )


def solution(mesh):
    in_specs = (
        P("pop", None, None),
        P("pop", "mp"),
        P("pop", "mp"),
        P("mp"),
        P("pop"),
        P("pop"),
        P("pop"),
    )
    out_specs = (P("pop", "mp"), P("pop", "mp"), P("pop"))
    body = functools.partial(shards, mesh.shape["mp"])
    return jax.shard_map(body, mesh=mesh, in_specs=in_specs, out_specs=out_specs, check_vma=False)
```

```python
import functools

import jax
import jax.numpy as jnp
from jax import lax
from jax.experimental import pallas as pl
from jax.experimental.pallas import tpu as pltpu
from jax.sharding import PartitionSpec as P

MESH = pl.DeviceIdType.MESH
SIGMA = 0.004
RATE = 0.0016
ROOT3 = 1.7320508075688772
ZED = 8
GROUP = 16

UP_LINK = [(0, 0, 0), (0, 0, 1), (-1, 0, 0), (0, 1, 1), (-2, 0, 0), (-1, 0, 1), (-3, 0, 0), (-1, 1, 1), (-2, 0, 1), (-2, 1, 1)]
DOWN_LINK = [(0, 0, 0), (0, 0, 1), (0, 1, 0), (1, 0, 1), (1, 0, 0), (2, 0, 1), (1, 1, 0), (3, 0, 1), (2, 0, 0), (2, 1, 0)]
SIDE_LINK = [(0, 0, 0), (0, 0, 1), (-1, 0, 0), (1, 0, 1), (-2, 0, 0), (2, 0, 1), (-3, 0, 0), (3, 0, 1), (-4, 0, 0), (4, 0, 1)]
SENDS = [UP_LINK, DOWN_LINK, SIDE_LINK]
ARRIVALS = [
    [(o - 1, w, h) for o, w, h in UP_LINK],
    [(o + 1, w, h) for o, w, h in DOWN_LINK],
    [(o, 1 - w, h) for o, w, h in SIDE_LINK],
]
STEPS = len(UP_LINK)


def same_piece(a, b):
    return (a[0] - b[0]) % ZED == 0 and a[1:] == b[1:]


def right_shift(v, amount):
    return lax.shift_right_logical(v, jnp.full_like(v, amount))


def mix(v):
    v = v ^ right_shift(v, 16)
    v = v * 2146121005
    v = v ^ right_shift(v, 15)
    v = v * -2073254261
    return v ^ right_shift(v, 16)


def anchor_of(seed, counter, slot):
    return mix(seed * 1103515245 + mix(counter * 668265263 + slot * 374761393))


def stream(anchor, position):
    h = mix(anchor + position * -1640531535)
    odd = (right_shift(h, 7) | 1) - 16777216
    return odd.astype(jnp.float32) * (ROOT3 / 16777216.0)


def kernel(
    mp_size, seeds, counters, ranks, prompts, gate_w, up_w, head,
    new_gate, new_up, scores,
    s_seeds, s_counters, s_ranks, v_head, xall, wbuf, acc, zbuf, lbuf, rbuf, vbuf, cbuf, ubuf, wown,
    s_own, s_sib, s_chip, s_side, s_all, r_own, r_sib, r_part, r_all, t_part, t_all,
    ring_s, ring_r, one_s, one_r, seed_s, seed_r, red_s, red_r, local_sem, word,
):
    rows, cols = gate_w.shape
    half = cols // 2
    tokens, width = prompts.shape
    members_here = seeds.shape[0]
    p = lax.axis_index("pop")
    m = lax.axis_index("mp")
    z = p // 4
    xl = lax.rem(p // 2, 2)
    c = lax.rem(p, 2)
    q = p // 2
    members_all = 128

    def pop_of(zz, xx, cc):
        return (zz * 2 + xx) * 2 + cc

    sibling = (pop_of(z, xl, 1 - c), m)
    up = (pop_of(lax.rem(z + 1, ZED), xl, c), m)
    down = (pop_of(lax.rem(z + ZED - 1, ZED), xl, c), m)
    side = (pop_of(z, 1 - xl, c), m)
    links = [up, down, side]

    def chip_peer(i):
        return (2 * lax.rem(q + i, GROUP) + c, m)

    def mp_peer(i):
        return (p, lax.rem(m + i, mp_size))

    ring = min(mp_size, 8)
    y = lax.rem(m, ring)
    base = m - y
    y_up = (p, base + lax.rem(y + 1, ring))
    y_down = (p, base + lax.rem(y + ring - 1, ring))
    across = (p, lax.rem(m + ring, mp_size))

    barrier = pltpu.get_barrier_semaphore()
    near = [sibling, up, down, side, y_up]
    if ring > 2:
        near.append(y_down)
    if mp_size > ring:
        near.append(across)
    for device in near:
        pl.semaphore_signal(barrier, inc=1, device_id=device, device_id_type=MESH)

    my_cols = pl.ds(pl.multiple_of(c * half, half), half)
    sib_cols = pl.ds(pl.multiple_of((1 - c) * half, half), half)
    own_rows = pl.ds(pl.multiple_of(c * tokens, tokens), tokens)
    keep_gate = pltpu.make_async_copy(gate_w.at[:, my_cols], wbuf.at[p, :, pl.ds(0, half)], local_sem.at[0])
    keep_up = pltpu.make_async_copy(up_w.at[:, my_cols], wbuf.at[p, :, pl.ds(half, half)], local_sem.at[1])
    keep_gate.start()
    keep_up.start()
    own_prompts = pltpu.make_async_copy(prompts, xall.at[own_rows], local_sem.at[2])
    own_prompts.start()
    load_gate = pltpu.make_async_copy(gate_w, wown.at[0], local_sem.at[3])
    load_up = pltpu.make_async_copy(up_w, wown.at[1], local_sem.at[4])
    load_gate.start()
    load_up.start()
    load_head = pltpu.make_async_copy(head, v_head, local_sem.at[5])
    load_head.start()
    ints = [(seeds, s_seeds), (counters, s_counters), (ranks, s_ranks)]
    load_ints = [pltpu.make_async_copy(a, b, local_sem.at[6 + i]) for i, (a, b) in enumerate(ints)]
    for load in load_ints:
        load.start()
    for load in load_ints:
        load.wait()

    lane = lax.broadcasted_iota(jnp.int32, (8, 128), 1)
    sub = lax.broadcasted_iota(jnp.int32, (8, 128), 0)
    block = jnp.zeros((8, 128), jnp.int32)
    for i in range(members_here):
        here = lane == p * members_here + i
        for row, values in enumerate((s_seeds, s_counters, s_ranks)):
            block = jnp.where(here & (sub == row), values[i], block)
    s_own[...] = block

    pl.semaphore_wait(barrier, len(near))

    def remote(src, dst, send, recv, device):
        return pltpu.make_async_remote_copy(
            src_ref=src, dst_ref=dst, send_sem=send, recv_sem=recv, device_id=device, device_id_type=MESH
        )

    give_gate = remote(gate_w.at[:, sib_cols], wbuf.at[p, :, pl.ds(0, half)], one_s.at[0], one_r.at[0], sibling)
    give_up = remote(up_w.at[:, sib_cols], wbuf.at[p, :, pl.ds(half, half)], one_s.at[1], one_r.at[1], sibling)
    give_seeds = remote(s_own, s_sib, one_s.at[2], one_r.at[2], sibling)
    give_prompts = remote(prompts, xall.at[own_rows], one_s.at[3], one_r.at[3], sibling)
    give_gate.start()
    give_up.start()
    give_seeds.start()

    def ring_copy(link, index):
        offset, other, core = SENDS[link][index]
        column = 1 - xl if other else xl
        where = pop_of(lax.rem(z + offset + 2 * ZED, ZED), column, 1 - c if core else c)
        piece = wbuf.at[where]
        return remote(piece, piece, ring_s.at[link, index], ring_r.at[link, index], links[link])

    def pass_on(piece):
        for link in range(3):
            for index, sent in enumerate(SENDS[link]):
                if same_piece(piece, sent):
                    ring_copy(link, index).start()

    def arrive(step):
        for link in range(3):
            ring_copy(link, step).wait_recv()
            pass_on(ARRIVALS[link][step])

    keep_gate.wait()
    keep_up.wait()
    for link in range(3):
        ring_copy(link, 0).start()
    give_gate.wait_recv()
    give_up.wait_recv()
    for link in range(3):
        ring_copy(link, 1).start()
    give_prompts.start()

    give_seeds.wait_recv()
    s_chip[...] = s_own[...] + s_sib[...]
    give_chip = remote(s_chip, s_side, one_s.at[5], one_r.at[5], side)
    give_chip.start()

    def seed_hop(step, act):
        for link, sign in ((0, -1), (1, 1)):
            if step < ZED // 2 - link:
                block = s_all.at[lax.rem(z + sign * step + ZED, ZED)]
                act(remote(block, block, seed_s.at[link, step], seed_r.at[link, step], links[link]))

    def start(copy):
        copy.start()

    def receive(copy):
        copy.wait_recv()

    def sent(copy):
        copy.wait_send()

    def pass_word():
        pl.semaphore_signal(word.at[0], inc=1, device_id=y_up, device_id_type=MESH)
        if ring > 2:
            pl.semaphore_signal(word.at[1], inc=1, device_id=y_down, device_id_type=MESH)

    def take_word():
        pl.semaphore_wait(word.at[0], 1)
        if ring > 2:
            pl.semaphore_wait(word.at[1], 1)

    def over_peers(act, count=GROUP):
        def step(i, carry):
            act(i)
            return carry

        lax.fori_loop(1, count, step, 0)

    def hash_members():
        pick = lane == q * 8 + sub
        columns = [
            jnp.sum(
                jnp.where(pick, anchor_of(s_chip[0:1, :], s_chip[1:2, :] + 1, slot), 0), axis=1, keepdims=True
            )
            for slot in range(4)
        ]
        wide = lax.broadcasted_iota(jnp.int32, (8, 1024), 1)
        for start in range(0, width, 1024):
            vbuf[0:8, start : start + 1024] = stream(columns[0], wide + start)
            vbuf[8:16, start : start + 1024] = stream(columns[2], wide + start)
        here = m * cols + c * half + lax.broadcasted_iota(jnp.int32, (8, half), 1)
        cbuf[0:8, :] = stream(columns[1], here) * SIGMA
        cbuf[8:16, :] = stream(columns[3], here) * SIGMA

    n_chunks = 4
    chunk = width // n_chunks

    def project(i):
        k = pl.ds(i * chunk, chunk)
        own = lax.dot_general(
            xall[:, k], vbuf[:, k].astype(jnp.bfloat16), (((1,), (1,)), ((), ())), preferred_element_type=jnp.float32
        )
        ubuf[:, 0:16] = own if i == 0 else ubuf[:, 0:16] + own

    seq = 2 * tokens // 8

    def rank_one():
        for i in range(8):
            r = slice(i * seq, (i + 1) * seq)
            for index in range(2):
                s = slice(index * half, (index + 1) * half)
                j = index * 8 + i
                acc[r, s] += ubuf[r, j : j + 1] * cbuf[j : j + 1, :]

    def multiply(offset, other=None, core=None):
        zz = lax.rem(z + offset + ZED, ZED)
        if other is None:
            first, count = pop_of(zz, 0, 0), 4
        elif core is None:
            first, count = pop_of(zz, 1 - xl if other else xl, 0), 2
        else:
            first, count = pop_of(zz, 1 - xl if other else xl, 1 - c if core else c), 1
        depth = count * rows
        k = pl.ds(pl.multiple_of(first * rows, depth), depth)
        w = wbuf[pl.ds(first, count)].reshape(depth, cols)
        acc[...] += jnp.dot(xall[:, k], w, preferred_element_type=jnp.float32)

    acc[...] = jnp.zeros_like(acc)
    pass_word()
    hash_members()
    arrive(0)
    take_word()
    give_chip.wait_recv()
    s_all[z] = s_chip[...] + s_side[...]
    seed_hop(0, start)
    pass_word()
    arrive(1)
    take_word()
    seed_hop(0, receive)
    seed_hop(1, start)
    pass_word()
    own_prompts.wait()
    arrive(2)
    take_word()
    seed_hop(1, receive)
    seed_hop(2, start)
    pass_word()
    give_prompts.wait_recv()
    project(0)
    project(1)
    multiply(0)
    arrive(3)
    take_word()
    seed_hop(2, receive)
    seed_hop(3, start)
    project(2)
    project(3)
    multiply(-1)
    arrive(4)
    seed_hop(3, receive)
    table = s_all[0]
    for i in range(1, ZED):
        table = table + s_all[i]
    seed_row = table[0:1, :]
    count_row = table[1:2, :]
    fit_row = (table[2:3, :].astype(jnp.float32) + 0.5) / members_all - 0.5
    left_gate = anchor_of(seed_row, count_row, 0)
    left_up = anchor_of(seed_row, count_row, 2)
    right_gate = anchor_of(seed_row, count_row, 1)
    right_up = anchor_of(seed_row, count_row, 3)
    scaling = RATE / (members_all * SIGMA)

    def hash_left(first, count):
        def step(i, carry):
            start = pl.multiple_of(i * 128, 128)
            position = start + lax.broadcasted_iota(jnp.int32, (128, 128), 0)
            lbuf[pl.ds(start, 128), 0:128] = (stream(left_gate, position) * fit_row).astype(jnp.bfloat16)
            lbuf[pl.ds(start, 128), 128:256] = (stream(left_up, position) * fit_row).astype(jnp.bfloat16)
            return carry

        lax.fori_loop(first, first + count, step, 0)

    def hash_right():
        def step(i, carry):
            start = pl.multiple_of(i * 128, 128)
            position = m * cols + start + lax.broadcasted_iota(jnp.int32, (128, 128), 0)
            rbuf[pl.ds(start, 128), 0:128] = stream(right_gate, position).astype(jnp.bfloat16)
            rbuf[pl.ds(start, 128), 128:256] = stream(right_up, position).astype(jnp.bfloat16)
            return carry

        lax.fori_loop(0, cols // 128, step, 0)

    def fresh_rows():
        own = pl.ds(pl.multiple_of(p * rows, rows), rows)
        load_gate.wait()
        load_up.wait()
        for index, out in enumerate((new_gate, new_up)):
            part = pl.ds(index * 128, 128)
            delta = lax.dot_general(
                lbuf[own, part], rbuf[:, part], (((1,), (1,)), ((), ())), preferred_element_type=jnp.float32
            )
            out[...] = (wown[index].astype(jnp.float32) + scaling * delta).astype(out.dtype)

    def low_rank(i):
        k = pl.ds(i * chunk, chunk)
        own = jnp.dot(xall[:, k], lbuf[k, :], preferred_element_type=jnp.float32)
        zbuf[...] = own if i == 0 else zbuf[...] + own

    def add_low_rank():
        for index in range(2):
            part = slice(index * 128, index * 128 + 128)
            acc[:, index * half : (index + 1) * half] += lax.dot_general(
                (zbuf[:, part] * scaling).astype(jnp.bfloat16),
                rbuf[pl.ds(pl.multiple_of(c * half, half), half), part],
                (((1,), (1,)), ((), ())),
                preferred_element_type=jnp.float32,
            )

    n_hash = width // 128
    hash_left(0, n_hash // 2)
    multiply(1)
    arrive(5)
    hash_left(n_hash // 2, n_hash // 2)
    hash_right()
    arrive(6)
    for i in range(n_chunks):
        low_rank(i)
    arrive(7)
    fresh_rows()
    add_low_rank()
    rank_one()
    multiply(2)
    multiply(4, 0)
    arrive(8)
    multiply(-2)
    multiply(-3, 0)
    multiply(3, 0)
    multiply(-3, 1, 0)
    multiply(3, 1, 1)
    multiply(-4, 1, 0)
    arrive(9)
    multiply(-3, 1, 1)
    multiply(3, 1, 0)
    multiply(4, 1, 1)

    load_head.wait()
    head_row = v_head[my_cols].astype(jnp.float32).reshape(1, half)
    parts = []
    for i in range(8):
        r = slice(i * seq, (i + 1) * seq)
        gate = acc[r, 0:half]
        value = gate / (1.0 + jnp.exp(-gate)) * acc[r, half:cols]
        parts.append(jnp.sum(value, axis=0, keepdims=True))
    summed = jnp.sum(jnp.concatenate(parts, axis=0) * head_row, axis=1, keepdims=True)
    r_own[...] = jnp.where(lane == q * 8 + sub, summed, 0.0)

    give_reward = remote(r_own, r_sib, one_s.at[4], one_r.at[4], sibling)
    give_reward.start()
    give_reward.wait_recv()
    r_part[...] = r_own[...] + r_sib[...]
    r_all[m] = r_part[...]

    def part_copy(i):
        return remote(r_part, r_all.at[m], red_s.at[0, i], red_r.at[0, i], mp_peer(i))

    over_peers(lambda i: part_copy(i).start(), mp_size)
    over_peers(lambda i: part_copy(i).wait_recv(), mp_size)
    t_part[...] = jnp.sum(r_all[...], axis=0)
    t_all[q] = t_part[...]

    def total_copy(i):
        return remote(t_part, t_all.at[q], red_s.at[1, i], red_r.at[1, i], chip_peer(i))

    over_peers(lambda i: total_copy(i).start())
    over_peers(lambda i: total_copy(i).wait_recv())
    rewards = jnp.sum(jnp.sum(t_all[...], axis=0), axis=0, keepdims=True) / seq
    mean = jnp.sum(rewards, axis=1, keepdims=True) / members_all
    spread = jnp.sum((rewards - mean) ** 2, axis=1, keepdims=True) / members_all
    result = (rewards - mean) / jnp.sqrt(spread + 1e-05)
    for i in range(members_here):
        scores[i] = jnp.sum(jnp.where(lane[0:1] == p * members_here + i, result, 0.0))

    give_gate.wait_send()
    give_up.wait_send()
    give_seeds.wait_send()
    give_prompts.wait_send()
    give_reward.wait_send()
    for link in range(3):
        for index in range(STEPS):
            ring_copy(link, index).wait_send()
    give_chip.wait_send()
    for step in range(ZED // 2):
        seed_hop(step, sent)
    over_peers(lambda i: part_copy(i).wait_send(), mp_size)
    over_peers(lambda i: total_copy(i).wait_send())


def finish(*refs):
    count = len(refs) // 2
    for source, target in zip(refs[:count], refs[count:]):
        target[...] = source[...]


def shards(mp_size, prompts, gate_weight, up_weight, reward_head, member_seeds, counters, member_ranks):
    members_here, seq, width = prompts.shape
    rows, cols = gate_weight.shape
    tokens = members_here * seq
    half = cols // 2
    hbm = pl.BlockSpec(memory_space=pltpu.HBM)
    vmem = pl.BlockSpec(memory_space=pltpu.VMEM)
    smem = pl.BlockSpec(memory_space=pltpu.SMEM)
    tile_f32 = pltpu.VMEM((8, 128), jnp.float32)
    tile_i32 = pltpu.VMEM((8, 128), jnp.int32)
    dma = pltpu.SemaphoreType.DMA
    results = pl.pallas_call(
        functools.partial(kernel, mp_size),
        out_shape=(
            jax.ShapeDtypeStruct((rows, cols), jnp.bfloat16),
            jax.ShapeDtypeStruct((rows, cols), jnp.bfloat16),
            jax.ShapeDtypeStruct((members_here,), jnp.float32),
        ),
        in_specs=[hbm] * 7,
        out_specs=(vmem, vmem, smem),
        scratch_shapes=[
            pltpu.SMEM((members_here,), jnp.int32),
            pltpu.SMEM((members_here,), jnp.int32),
            pltpu.SMEM((members_here,), jnp.int32),
            pltpu.VMEM((cols,), jnp.bfloat16),
            pltpu.VMEM((2 * tokens, width), jnp.bfloat16),
            pltpu.VMEM((2 * GROUP, rows, cols), jnp.bfloat16),
            pltpu.VMEM((2 * tokens, cols), jnp.float32),
            pltpu.VMEM((2 * tokens, 256), jnp.float32),
            pltpu.VMEM((width, 256), jnp.bfloat16),
            pltpu.VMEM((cols, 256), jnp.bfloat16),
            pltpu.VMEM((16, width), jnp.float32),
            pltpu.VMEM((16, half), jnp.float32),
            pltpu.VMEM((2 * tokens, 128), jnp.float32),
            pltpu.VMEM((2, rows, cols), jnp.bfloat16),
            tile_i32,
            tile_i32,
            tile_i32,
            tile_i32,
            pltpu.VMEM((ZED, 8, 128), jnp.int32),
            tile_f32,
            tile_f32,
            tile_f32,
            pltpu.VMEM((mp_size, 8, 128), jnp.float32),
            tile_f32,
            pltpu.VMEM((GROUP, 8, 128), jnp.float32),
            dma((3, STEPS)),
            dma((3, STEPS)),
            dma((6,)),
            dma((6,)),
            dma((2, ZED // 2)),
            dma((2, ZED // 2)),
            dma((2, GROUP)),
            dma((2, GROUP)),
            dma((9,)),
            pltpu.SemaphoreType.REGULAR((2,)),
        ],
        compiler_params=pltpu.CompilerParams(
            collective_id=0, has_side_effects=True, vmem_limit_bytes=60 * 1024 * 1024
        ),
        name="generation",
    )(
        member_seeds,
        counters,
        member_ranks,
        prompts.reshape(tokens, width),
        gate_weight,
        up_weight,
        reward_head,
    )
    return pl.pallas_call(
        finish,
        out_shape=tuple(jax.ShapeDtypeStruct(r.shape, r.dtype) for r in results),
        in_specs=[vmem] * 3,
        out_specs=(vmem,) * 3,
        compiler_params=pltpu.CompilerParams(vmem_limit_bytes=60 * 1024 * 1024),
        name="finish",
    )(*results)


def solution(mesh):
    in_specs = (
        P("pop", None, None),
        P("pop", "mp"),
        P("pop", "mp"),
        P("mp"),
        P("pop"),
        P("pop"),
        P("pop"),
    )
    out_specs = (P("pop", "mp"), P("pop", "mp"), P("pop"))
    body = functools.partial(shards, mesh.shape["mp"])
    return jax.shard_map(body, mesh=mesh, in_specs=in_specs, out_specs=out_specs, check_vma=False)
```

```python
import functools

import jax
import jax.numpy as jnp
from jax import lax
from jax.experimental import pallas as pl
from jax.experimental.pallas import tpu as pltpu
from jax.sharding import PartitionSpec as P

MESH = pl.DeviceIdType.MESH
SIGMA = 0.004
RATE = 0.0016
ROOT3 = 1.7320508075688772
ZED = 8
GROUP = 16

UP_LINK = [(0, 0, 0), (0, 0, 1), (-1, 0, 0), (0, 1, 1), (-2, 0, 0), (-1, 0, 1), (-3, 0, 0), (-1, 1, 1), (-2, 0, 1), (-2, 1, 1)]
DOWN_LINK = [(0, 0, 0), (0, 0, 1), (0, 1, 0), (1, 0, 1), (1, 0, 0), (2, 0, 1), (1, 1, 0), (3, 0, 1), (2, 0, 0), (2, 1, 0)]
SIDE_LINK = [(0, 0, 0), (0, 0, 1), (-1, 0, 0), (1, 0, 1), (-2, 0, 0), (2, 0, 1), (-3, 0, 0), (3, 0, 1), (-4, 0, 0), (4, 0, 1)]
SENDS = [UP_LINK, DOWN_LINK, SIDE_LINK]
ARRIVALS = [
    [(o - 1, w, h) for o, w, h in UP_LINK],
    [(o + 1, w, h) for o, w, h in DOWN_LINK],
    [(o, 1 - w, h) for o, w, h in SIDE_LINK],
]
STEPS = len(UP_LINK)


def same_piece(a, b):
    return (a[0] - b[0]) % ZED == 0 and a[1:] == b[1:]


def right_shift(v, amount):
    return lax.shift_right_logical(v, jnp.full_like(v, amount))


def mix(v):
    v = v ^ right_shift(v, 16)
    v = v * 2146121005
    v = v ^ right_shift(v, 15)
    v = v * -2073254261
    return v ^ right_shift(v, 16)


def anchor_of(seed, counter, slot):
    return mix(seed * 1103515245 + mix(counter * 668265263 + slot * 374761393))


def stream(anchor, position):
    h = mix(anchor + position * -1640531535)
    odd = (right_shift(h, 7) | 1) - 16777216
    return odd.astype(jnp.float32) * (ROOT3 / 16777216.0)


def kernel(
    mp_size, seeds, counters, ranks, prompts, gate_w, up_w, head,
    new_gate, new_up, scores,
    s_seeds, s_counters, s_ranks, v_head, xall, wbuf, acc, z_own, z_sib, lbuf, lown, rbuf, vbuf, cbuf, wown,
    s_own, s_sib, s_chip, s_side, s_all, r_own, r_sib, r_part, r_all, t_part, t_all,
    ring_s, ring_r, one_s, one_r, seed_s, seed_r, red_s, red_r, local_sem, word,
):
    rows, cols = gate_w.shape
    half = cols // 2
    tokens, width = prompts.shape
    members_here = seeds.shape[0]
    p = lax.axis_index("pop")
    m = lax.axis_index("mp")
    z = p // 4
    xl = lax.rem(p // 2, 2)
    c = lax.rem(p, 2)
    q = p // 2
    members_all = 128

    def pop_of(zz, xx, cc):
        return (zz * 2 + xx) * 2 + cc

    sibling = (pop_of(z, xl, 1 - c), m)
    up = (pop_of(lax.rem(z + 1, ZED), xl, c), m)
    down = (pop_of(lax.rem(z + ZED - 1, ZED), xl, c), m)
    side = (pop_of(z, 1 - xl, c), m)
    links = [up, down, side]

    def by_distance(count, sides):
        pairs = [(o, w) for o in range(count) for w in range(sides) if o or w]
        return sorted(pairs, key=lambda pair: -min(pair[0], count - pair[0]))

    chip_pairs = by_distance(ZED, 2)

    def chip_peer(i):
        o, w = chip_pairs[i]
        return (pop_of(lax.rem(z + o, ZED), 1 - xl if w else xl, c), m)

    ring = min(mp_size, 8)
    y = lax.rem(m, ring)
    base = m - y
    y_up = (p, base + lax.rem(y + 1, ring))
    y_down = (p, base + lax.rem(y + ring - 1, ring))
    across = (p, lax.rem(m + ring, mp_size))

    mp_pairs = by_distance(ring, mp_size // ring)

    def mp_peer(i):
        o, w = mp_pairs[i]
        return (p, lax.rem((base + ring if w else base), mp_size) + lax.rem(y + o, ring))

    barrier = pltpu.get_barrier_semaphore()
    near = [sibling, up, down, side, y_up]
    if ring > 2:
        near.append(y_down)
    if mp_size > ring:
        near.append(across)
    for device in near:
        pl.semaphore_signal(barrier, inc=1, device_id=device, device_id_type=MESH)

    my_cols = pl.ds(pl.multiple_of(c * half, half), half)
    sib_cols = pl.ds(pl.multiple_of((1 - c) * half, half), half)
    own_rows = pl.ds(pl.multiple_of(c * tokens, tokens), tokens)
    keep_gate = pltpu.make_async_copy(gate_w.at[:, my_cols], wbuf.at[p, :, pl.ds(0, half)], local_sem.at[0])
    keep_up = pltpu.make_async_copy(up_w.at[:, my_cols], wbuf.at[p, :, pl.ds(half, half)], local_sem.at[1])
    keep_gate.start()
    keep_up.start()
    own_prompts = pltpu.make_async_copy(prompts, xall.at[own_rows], local_sem.at[2])
    own_prompts.start()
    load_gate = pltpu.make_async_copy(gate_w, wown.at[0], local_sem.at[3])
    load_up = pltpu.make_async_copy(up_w, wown.at[1], local_sem.at[4])
    load_gate.start()
    load_up.start()
    load_head = pltpu.make_async_copy(head, v_head, local_sem.at[5])
    load_head.start()
    ints = [(seeds, s_seeds), (counters, s_counters), (ranks, s_ranks)]
    load_ints = [pltpu.make_async_copy(a, b, local_sem.at[6 + i]) for i, (a, b) in enumerate(ints)]
    for load in load_ints:
        load.start()
    for load in load_ints:
        load.wait()

    lane = lax.broadcasted_iota(jnp.int32, (8, 128), 1)
    sub = lax.broadcasted_iota(jnp.int32, (8, 128), 0)
    block = jnp.zeros((8, 128), jnp.int32)
    for i in range(members_here):
        here = lane == p * members_here + i
        for row, values in enumerate((s_seeds, s_counters, s_ranks)):
            block = jnp.where(here & (sub == row), values[i], block)
    s_own[...] = block

    pl.semaphore_wait(barrier, len(near))

    def remote(src, dst, send, recv, device):
        return pltpu.make_async_remote_copy(
            src_ref=src, dst_ref=dst, send_sem=send, recv_sem=recv, device_id=device, device_id_type=MESH
        )

    give_gate = remote(gate_w.at[:, sib_cols], wbuf.at[p, :, pl.ds(0, half)], one_s.at[0], one_r.at[0], sibling)
    give_up = remote(up_w.at[:, sib_cols], wbuf.at[p, :, pl.ds(half, half)], one_s.at[1], one_r.at[1], sibling)
    give_seeds = remote(s_own, s_sib, one_s.at[2], one_r.at[2], sibling)
    give_prompts = remote(prompts, xall.at[own_rows], one_s.at[3], one_r.at[3], sibling)
    give_gate.start()
    give_up.start()
    give_seeds.start()

    def ring_copy(link, index):
        offset, other, core = SENDS[link][index]
        column = 1 - xl if other else xl
        where = pop_of(lax.rem(z + offset + 2 * ZED, ZED), column, 1 - c if core else c)
        piece = wbuf.at[where]
        return remote(piece, piece, ring_s.at[link, index], ring_r.at[link, index], links[link])

    def pass_on(piece):
        for link in range(3):
            for index, sent in enumerate(SENDS[link]):
                if same_piece(piece, sent):
                    ring_copy(link, index).start()

    def arrive(step):
        for link in range(3):
            ring_copy(link, step).wait_recv()
            pass_on(ARRIVALS[link][step])

    keep_gate.wait()
    keep_up.wait()
    for link in range(3):
        ring_copy(link, 0).start()
    give_gate.wait_recv()
    give_up.wait_recv()
    for link in range(3):
        ring_copy(link, 1).start()
    give_prompts.start()

    give_seeds.wait_recv()
    s_chip[...] = s_own[...] + s_sib[...]
    give_chip = remote(s_chip, s_side, one_s.at[5], one_r.at[5], side)
    give_chip.start()

    def seed_hop(step, act):
        for link, sign in ((0, -1), (1, 1)):
            if step < ZED // 2 - link:
                block = s_all.at[lax.rem(z + sign * step + ZED, ZED)]
                act(remote(block, block, seed_s.at[link, step], seed_r.at[link, step], links[link]))

    def start(copy):
        copy.start()

    def receive(copy):
        copy.wait_recv()

    def sent(copy):
        copy.wait_send()

    def pass_word():
        pl.semaphore_signal(word.at[0], inc=1, device_id=y_up, device_id_type=MESH)
        if ring > 2:
            pl.semaphore_signal(word.at[1], inc=1, device_id=y_down, device_id_type=MESH)

    def take_word():
        pl.semaphore_wait(word.at[0], 1)
        if ring > 2:
            pl.semaphore_wait(word.at[1], 1)

    n_chunks = 2
    chunk = width // 2 // n_chunks

    def width_part(i):
        return pl.ds(pl.multiple_of((c * n_chunks + i) * chunk, chunk), chunk)

    def hash_members():
        pick = lane == q * 8 + sub
        columns = [
            jnp.sum(
                jnp.where(pick, anchor_of(s_chip[0:1, :], s_chip[1:2, :] + 1, slot), 0), axis=1, keepdims=True
            )
            for slot in range(4)
        ]
        wide = lax.broadcasted_iota(jnp.int32, (8, chunk), 1)
        for i in range(n_chunks):
            first = (c * n_chunks + i) * chunk
            vbuf[0:8, i * chunk : (i + 1) * chunk] = stream(columns[0], wide + first)
            vbuf[8:16, i * chunk : (i + 1) * chunk] = stream(columns[2], wide + first)
        here = m * cols + c * half + lax.broadcasted_iota(jnp.int32, (8, half), 1)
        cbuf[0:8, :] = stream(columns[1], here) * SIGMA
        cbuf[8:16, :] = stream(columns[3], here) * SIGMA

    def project(i):
        own = lax.dot_general(
            xall[:, width_part(i)],
            vbuf[:, i * chunk : (i + 1) * chunk].astype(jnp.bfloat16),
            (((1,), (1,)), ((), ())),
            preferred_element_type=jnp.float32,
        )
        z_own[:, 256:272] = own if i == 0 else z_own[:, 256:272] + own

    seq = 2 * tokens // 8

    def rank_one():
        for i in range(8):
            r = slice(i * seq, (i + 1) * seq)
            for index in range(2):
                s = slice(index * half, (index + 1) * half)
                j = index * 8 + i
                along = z_own[r, 256 + j : 257 + j] + z_sib[r, 256 + j : 257 + j]
                acc[r, s] += along * cbuf[j : j + 1, :]

    def block_of(offset, other, core):
        zz = lax.rem(z + offset + ZED, ZED)
        return pop_of(zz, 1 - xl if other else xl, 1 - c if core else c)

    def multiply(*pieces):
        firsts = [block_of(*piece) for piece in pieces]
        ks = [pl.ds(pl.multiple_of(first * rows, rows), rows) for first in firsts]
        x = jnp.concatenate([xall[:, k] for k in ks], axis=1) if len(ks) > 1 else xall[:, ks[0]]
        w = jnp.concatenate([wbuf[first] for first in firsts], axis=0) if len(ks) > 1 else wbuf[firsts[0]]
        acc[...] += jnp.dot(x, w, preferred_element_type=jnp.float32)

    def multiply_chip(offset, other=None):
        zz = lax.rem(z + offset + ZED, ZED)
        if other is None:
            first, count = pop_of(zz, 0, 0), 4
        else:
            first, count = pop_of(zz, 1 - xl if other else xl, 0), 2
        depth = count * rows
        k = pl.ds(pl.multiple_of(first * rows, depth), depth)
        w = wbuf[pl.ds(first, count)].reshape(depth, cols)
        acc[...] += jnp.dot(xall[:, k], w, preferred_element_type=jnp.float32)

    acc[...] = jnp.zeros_like(acc)
    pass_word()
    hash_members()
    arrive(0)
    take_word()
    give_chip.wait_recv()
    s_all[z] = s_chip[...] + s_side[...]
    seed_hop(0, start)
    pass_word()
    arrive(1)
    take_word()
    seed_hop(0, receive)
    seed_hop(1, start)
    pass_word()
    own_prompts.wait()
    arrive(2)
    take_word()
    seed_hop(1, receive)
    seed_hop(2, start)
    pass_word()
    give_prompts.wait_recv()
    project(0)
    multiply_chip(0)
    arrive(3)
    take_word()
    seed_hop(2, receive)
    seed_hop(3, start)
    project(1)
    multiply_chip(-1)
    arrive(4)
    seed_hop(3, receive)
    table = s_all[0]
    for i in range(1, ZED):
        table = table + s_all[i]
    seed_row = table[0:1, :]
    count_row = table[1:2, :]
    fit_row = (table[2:3, :].astype(jnp.float32) + 0.5) / members_all - 0.5
    left_gate = anchor_of(seed_row, count_row, 0)
    left_up = anchor_of(seed_row, count_row, 2)
    right_gate = anchor_of(seed_row, count_row, 1)
    right_up = anchor_of(seed_row, count_row, 3)
    scaling = RATE / (members_all * SIGMA)

    def hash_left(row, target, start):
        position = row + lax.broadcasted_iota(jnp.int32, (128, 128), 0)
        target[pl.ds(start, 128), 0:128] = (stream(left_gate, position) * fit_row).astype(jnp.bfloat16)
        target[pl.ds(start, 128), 128:256] = (stream(left_up, position) * fit_row).astype(jnp.bfloat16)

    def hash_width(first, count):
        def step(i, carry):
            hash_left(c * (width // 2) + i * 128, lbuf, pl.multiple_of(i * 128, 128))
            return carry

        lax.fori_loop(first, first + count, step, 0)

    def hash_right():
        def step(i, carry):
            start = pl.multiple_of(i * 128, 128)
            position = m * cols + start + lax.broadcasted_iota(jnp.int32, (128, 128), 0)
            rbuf[pl.ds(start, 128), 0:128] = stream(right_gate, position).astype(jnp.bfloat16)
            rbuf[pl.ds(start, 128), 128:256] = stream(right_up, position).astype(jnp.bfloat16)
            return carry

        lax.fori_loop(0, cols // 128, step, 0)

    def fresh_rows():
        hash_left(p * rows, lown, 0)
        load_gate.wait()
        load_up.wait()
        for index, out in enumerate((new_gate, new_up)):
            part = pl.ds(index * 128, 128)
            delta = lax.dot_general(
                lown[:, part], rbuf[:, part], (((1,), (1,)), ((), ())), preferred_element_type=jnp.float32
            )
            out[...] = (wown[index].astype(jnp.float32) + scaling * delta).astype(out.dtype)

    def low_rank(i):
        own = jnp.dot(xall[:, width_part(i)], lbuf[i * chunk : (i + 1) * chunk, :], preferred_element_type=jnp.float32)
        z_own[:, 0:256] = own if i == 0 else z_own[:, 0:256] + own

    def add_low_rank():
        for index in range(2):
            part = slice(index * 128, index * 128 + 128)
            acc[:, index * half : (index + 1) * half] += lax.dot_general(
                ((z_own[:, part] + z_sib[:, part]) * scaling).astype(jnp.bfloat16),
                rbuf[pl.ds(pl.multiple_of(c * half, half), half), part],
                (((1,), (1,)), ((), ())),
                preferred_element_type=jnp.float32,
            )

    give_low = remote(z_own, z_sib, one_s.at[6], one_r.at[6], sibling)
    n_hash = width // 2 // 128
    hash_width(0, n_hash)
    arrive(5)
    for i in range(n_chunks):
        low_rank(i)
    give_low.start()
    multiply_chip(1)
    arrive(6)
    hash_right()
    fresh_rows()
    give_low.wait_recv()
    add_low_rank()
    arrive(7)
    rank_one()
    multiply_chip(2)
    multiply_chip(4, 0)
    arrive(8)
    multiply_chip(-2)
    multiply_chip(-3, 0)
    multiply_chip(3, 0)
    multiply((-3, 1, 0), (3, 1, 1), (4, 1, 0))
    arrive(9)
    multiply((-3, 1, 1), (3, 1, 0), (4, 1, 1))

    load_head.wait()
    head_row = v_head[my_cols].astype(jnp.float32).reshape(1, half)
    parts = []
    for i in range(8):
        r = slice(i * seq, (i + 1) * seq)
        gate = acc[r, 0:half]
        value = gate / (1.0 + jnp.exp(-gate)) * acc[r, half:cols]
        parts.append(jnp.sum(value, axis=0, keepdims=True))
    summed = jnp.sum(jnp.concatenate(parts, axis=0) * head_row, axis=1, keepdims=True)
    r_own[...] = jnp.where(lane == q * 8 + sub, summed, 0.0)

    give_reward = remote(r_own, r_sib, one_s.at[4], one_r.at[4], sibling)
    give_reward.start()
    give_reward.wait_recv()
    r_part[...] = r_own[...] + r_sib[...]
    r_all[m] = r_part[...]

    def part_copy(i):
        return remote(r_part, r_all.at[m], red_s.at[0, i], red_r.at[0, i], mp_peer(i))

    for i in range(len(mp_pairs)):
        part_copy(i).start()
    for i in range(len(mp_pairs)):
        part_copy(i).wait_recv()
    t_part[...] = jnp.sum(r_all[...], axis=0)
    t_all[q] = t_part[...]

    def total_copy(i):
        return remote(t_part, t_all.at[q], red_s.at[1, i], red_r.at[1, i], chip_peer(i))

    for i in range(len(chip_pairs)):
        total_copy(i).start()
    for i in range(len(chip_pairs)):
        total_copy(i).wait_recv()
    rewards = jnp.sum(jnp.sum(t_all[...], axis=0), axis=0, keepdims=True) / seq
    mean = jnp.sum(rewards, axis=1, keepdims=True) / members_all
    spread = jnp.sum((rewards - mean) ** 2, axis=1, keepdims=True) / members_all
    result = (rewards - mean) / jnp.sqrt(spread + 1e-05)
    scores[...] = jnp.broadcast_to(result, scores.shape)

    give_gate.wait_send()
    give_up.wait_send()
    give_seeds.wait_send()
    give_prompts.wait_send()
    give_reward.wait_send()
    for link in range(3):
        for index in range(STEPS):
            ring_copy(link, index).wait_send()
    give_chip.wait_send()
    give_low.wait_send()
    for step in range(ZED // 2):
        seed_hop(step, sent)
    for i in range(len(mp_pairs)):
        part_copy(i).wait_send()
    for i in range(len(chip_pairs)):
        total_copy(i).wait_send()


def finish(gate, up, all_scores, new_gate, new_up, scores):
    new_gate[...] = gate[...]
    new_up[...] = up[...]
    first = lax.axis_index("pop") * scores.shape[0]
    lane = lax.broadcasted_iota(jnp.int32, all_scores.shape, 1)
    sub = lax.broadcasted_iota(jnp.int32, all_scores.shape, 0)
    for i in range(scores.shape[0]):
        scores[i] = jnp.sum(jnp.where((lane == first + i) & (sub == 0), all_scores[...], 0.0))


def shards(mp_size, prompts, gate_weight, up_weight, reward_head, member_seeds, counters, member_ranks):
    members_here, seq, width = prompts.shape
    rows, cols = gate_weight.shape
    tokens = members_here * seq
    half = cols // 2
    hbm = pl.BlockSpec(memory_space=pltpu.HBM)
    vmem = pl.BlockSpec(memory_space=pltpu.VMEM)
    smem = pl.BlockSpec(memory_space=pltpu.SMEM)
    tile_f32 = pltpu.VMEM((8, 128), jnp.float32)
    tile_i32 = pltpu.VMEM((8, 128), jnp.int32)
    dma = pltpu.SemaphoreType.DMA
    results = pl.pallas_call(
        functools.partial(kernel, mp_size),
        out_shape=(
            pltpu.VMEM((rows, cols), jnp.bfloat16),
            pltpu.VMEM((rows, cols), jnp.bfloat16),
            pltpu.VMEM((8, 128), jnp.float32),
        ),
        in_specs=[hbm] * 7,
        out_specs=(vmem,) * 3,
        scratch_shapes=[
            pltpu.SMEM((members_here,), jnp.int32),
            pltpu.SMEM((members_here,), jnp.int32),
            pltpu.SMEM((members_here,), jnp.int32),
            pltpu.VMEM((cols,), jnp.bfloat16),
            pltpu.VMEM((2 * tokens, width), jnp.bfloat16),
            pltpu.VMEM((2 * GROUP, rows, cols), jnp.bfloat16),
            pltpu.VMEM((2 * tokens, cols), jnp.float32),
            pltpu.VMEM((2 * tokens, 384), jnp.float32),
            pltpu.VMEM((2 * tokens, 384), jnp.float32),
            pltpu.VMEM((width // 2, 256), jnp.bfloat16),
            pltpu.VMEM((rows, 256), jnp.bfloat16),
            pltpu.VMEM((cols, 256), jnp.bfloat16),
            pltpu.VMEM((16, width // 2), jnp.float32),
            pltpu.VMEM((16, half), jnp.float32),
            pltpu.VMEM((2, rows, cols), jnp.bfloat16),
            tile_i32,
            tile_i32,
            tile_i32,
            tile_i32,
            pltpu.VMEM((ZED, 8, 128), jnp.int32),
            tile_f32,
            tile_f32,
            tile_f32,
            pltpu.VMEM((mp_size, 8, 128), jnp.float32),
            tile_f32,
            pltpu.VMEM((GROUP, 8, 128), jnp.float32),
            dma((3, STEPS)),
            dma((3, STEPS)),
            dma((7,)),
            dma((7,)),
            dma((2, ZED // 2)),
            dma((2, ZED // 2)),
            dma((2, GROUP)),
            dma((2, GROUP)),
            dma((9,)),
            pltpu.SemaphoreType.REGULAR((2,)),
        ],
        compiler_params=pltpu.CompilerParams(
            collective_id=0, has_side_effects=True, vmem_limit_bytes=60 * 1024 * 1024
        ),
        name="generation",
    )(
        member_seeds,
        counters,
        member_ranks,
        prompts.reshape(tokens, width),
        gate_weight,
        up_weight,
        reward_head,
    )
    return pl.pallas_call(
        finish,
        out_shape=(
            jax.ShapeDtypeStruct((rows, cols), jnp.bfloat16),
            jax.ShapeDtypeStruct((rows, cols), jnp.bfloat16),
            jax.ShapeDtypeStruct((members_here,), jnp.float32),
        ),
        in_specs=[vmem] * 3,
        out_specs=(vmem, vmem, smem),
        compiler_params=pltpu.CompilerParams(vmem_limit_bytes=8 * 1024 * 1024),
        name="finish",
    )(*results)


def solution(mesh):
    in_specs = (
        P("pop", None, None),
        P("pop", "mp"),
        P("pop", "mp"),
        P("mp"),
        P("pop"),
        P("pop"),
        P("pop"),
    )
    out_specs = (P("pop", "mp"), P("pop", "mp"), P("pop"))
    body = functools.partial(shards, mesh.shape["mp"])
    return jax.shard_map(body, mesh=mesh, in_specs=in_specs, out_specs=out_specs, check_vma=False)
```

```python
import functools

import jax
import jax.numpy as jnp
from jax import lax
from jax.experimental import pallas as pl
from jax.experimental.pallas import tpu as pltpu
from jax.sharding import PartitionSpec as P

MESH = pl.DeviceIdType.MESH
SIGMA = 0.004
RATE = 0.0016
ROOT3 = 1.7320508075688772
ZED = 8
GROUP = 16

UP_LINK = [(0, 0, 0), (0, 0, 1), (-1, 0, 0), (0, 1, 1), (-2, 0, 0), (-1, 0, 1), (-3, 0, 0), (-1, 1, 1), (-2, 0, 1), (-2, 1, 1)]
DOWN_LINK = [(0, 0, 0), (0, 0, 1), (0, 1, 0), (1, 0, 1), (1, 0, 0), (2, 0, 1), (1, 1, 0), (3, 0, 1), (2, 0, 0), (2, 1, 0)]
SIDE_LINK = [(0, 0, 0), (0, 0, 1), (-1, 0, 0), (1, 0, 1), (-2, 0, 0), (2, 0, 1), (-3, 0, 0), (3, 0, 1), (-4, 0, 0), (4, 0, 1)]
SENDS = [UP_LINK, DOWN_LINK, SIDE_LINK]
ARRIVALS = [
    [(o - 1, w, h) for o, w, h in UP_LINK],
    [(o + 1, w, h) for o, w, h in DOWN_LINK],
    [(o, 1 - w, h) for o, w, h in SIDE_LINK],
]
STEPS = len(UP_LINK)


def same_piece(a, b):
    return (a[0] - b[0]) % ZED == 0 and a[1:] == b[1:]


def right_shift(v, amount):
    return lax.shift_right_logical(v, jnp.full_like(v, amount))


def mix(v):
    v = v ^ right_shift(v, 16)
    v = v * 2146121005
    v = v ^ right_shift(v, 15)
    v = v * -2073254261
    return v ^ right_shift(v, 16)


def anchor_of(seed, counter, slot):
    return mix(seed * 1103515245 + mix(counter * 668265263 + slot * 374761393))


def stream(anchor, position):
    h = mix(anchor + position * -1640531535)
    odd = (right_shift(h, 7) | 1) - 16777216
    return odd.astype(jnp.float32) * (ROOT3 / 16777216.0)


def kernel(
    mp_size, seeds, counters, ranks, prompts, gate_w, up_w, head,
    new_gate, new_up, scores,
    s_seeds, s_counters, s_ranks, v_head, xall, wbuf, acc, z_own, z_sib, u_own, u_sib, lbuf, lown, rbuf, vbuf, cbuf, wown,
    s_own, s_sib, s_chip, s_side, s_all, r_own, r_sib, r_part, r_all, t_part, t_all,
    ring_s, ring_r, one_s, one_r, seed_s, seed_r, red_s, red_r, local_sem, word,
):
    rows, cols = gate_w.shape
    half = cols // 2
    tokens, width = prompts.shape
    members_here = seeds.shape[0]
    p = lax.axis_index("pop")
    m = lax.axis_index("mp")
    z = p // 4
    xl = lax.rem(p // 2, 2)
    c = lax.rem(p, 2)
    q = p // 2
    members_all = 128

    def pop_of(zz, xx, cc):
        return (zz * 2 + xx) * 2 + cc

    sibling = (pop_of(z, xl, 1 - c), m)
    up = (pop_of(lax.rem(z + 1, ZED), xl, c), m)
    down = (pop_of(lax.rem(z + ZED - 1, ZED), xl, c), m)
    side = (pop_of(z, 1 - xl, c), m)
    links = [up, down, side]

    def by_distance(count, sides):
        pairs = [(o, w) for o in range(count) for w in range(sides) if o or w]
        return sorted(pairs, key=lambda pair: -min(pair[0], count - pair[0]))

    chip_pairs = by_distance(ZED, 2)

    def chip_peer(i):
        o, w = chip_pairs[i]
        return (pop_of(lax.rem(z + o, ZED), 1 - xl if w else xl, c), m)

    ring = min(mp_size, 8)
    y = lax.rem(m, ring)
    base = m - y
    y_up = (p, base + lax.rem(y + 1, ring))
    y_down = (p, base + lax.rem(y + ring - 1, ring))
    across = (p, lax.rem(m + ring, mp_size))

    mp_pairs = by_distance(ring, mp_size // ring)

    def mp_peer(i):
        o, w = mp_pairs[i]
        return (p, lax.rem((base + ring if w else base), mp_size) + lax.rem(y + o, ring))

    barrier = pltpu.get_barrier_semaphore()
    near = [sibling, up, down, side, y_up]
    if ring > 2:
        near.append(y_down)
    if mp_size > ring:
        near.append(across)
    for device in near:
        pl.semaphore_signal(barrier, inc=1, device_id=device, device_id_type=MESH)

    my_cols = pl.ds(pl.multiple_of(c * half, half), half)
    sib_cols = pl.ds(pl.multiple_of((1 - c) * half, half), half)
    own_rows = pl.ds(pl.multiple_of(c * tokens, tokens), tokens)
    keep_gate = pltpu.make_async_copy(gate_w.at[:, my_cols], wbuf.at[p, :, pl.ds(0, half)], local_sem.at[0])
    keep_up = pltpu.make_async_copy(up_w.at[:, my_cols], wbuf.at[p, :, pl.ds(half, half)], local_sem.at[1])
    keep_gate.start()
    keep_up.start()
    own_prompts = pltpu.make_async_copy(prompts, xall.at[own_rows], local_sem.at[2])
    own_prompts.start()
    load_gate = pltpu.make_async_copy(gate_w, wown.at[0], local_sem.at[3])
    load_up = pltpu.make_async_copy(up_w, wown.at[1], local_sem.at[4])
    load_gate.start()
    load_up.start()
    load_head = pltpu.make_async_copy(head, v_head, local_sem.at[5])
    load_head.start()
    ints = [(seeds, s_seeds), (counters, s_counters), (ranks, s_ranks)]
    load_ints = [pltpu.make_async_copy(a, b, local_sem.at[6 + i]) for i, (a, b) in enumerate(ints)]
    for load in load_ints:
        load.start()
    for load in load_ints:
        load.wait()

    lane = lax.broadcasted_iota(jnp.int32, (8, 128), 1)
    sub = lax.broadcasted_iota(jnp.int32, (8, 128), 0)
    block = jnp.zeros((8, 128), jnp.int32)
    for i in range(members_here):
        here = lane == p * members_here + i
        for row, values in enumerate((s_seeds, s_counters, s_ranks)):
            block = jnp.where(here & (sub == row), values[i], block)
    s_own[...] = block

    pl.semaphore_wait(barrier, len(near))

    def remote(src, dst, send, recv, device):
        return pltpu.make_async_remote_copy(
            src_ref=src, dst_ref=dst, send_sem=send, recv_sem=recv, device_id=device, device_id_type=MESH
        )

    give_gate = remote(gate_w.at[:, sib_cols], wbuf.at[p, :, pl.ds(0, half)], one_s.at[0], one_r.at[0], sibling)
    give_up = remote(up_w.at[:, sib_cols], wbuf.at[p, :, pl.ds(half, half)], one_s.at[1], one_r.at[1], sibling)
    give_seeds = remote(s_own, s_sib, one_s.at[2], one_r.at[2], sibling)
    give_prompts = remote(prompts, xall.at[own_rows], one_s.at[3], one_r.at[3], sibling)
    give_gate.start()
    give_up.start()
    give_seeds.start()

    def ring_copy(link, index):
        offset, other, core = SENDS[link][index]
        column = 1 - xl if other else xl
        where = pop_of(lax.rem(z + offset + 2 * ZED, ZED), column, 1 - c if core else c)
        piece = wbuf.at[where]
        return remote(piece, piece, ring_s.at[link, index], ring_r.at[link, index], links[link])

    def pass_on(piece):
        for link in range(3):
            for index, sent in enumerate(SENDS[link]):
                if same_piece(piece, sent):
                    ring_copy(link, index).start()

    def arrive(step):
        for link in range(3):
            ring_copy(link, step).wait_recv()
            pass_on(ARRIVALS[link][step])

    keep_gate.wait()
    keep_up.wait()
    for link in range(3):
        ring_copy(link, 0).start()
    give_gate.wait_recv()
    give_up.wait_recv()
    for link in range(3):
        ring_copy(link, 1).start()
    give_prompts.start()

    give_seeds.wait_recv()
    s_chip[...] = s_own[...] + s_sib[...]
    give_chip = remote(s_chip, s_side, one_s.at[5], one_r.at[5], side)
    give_chip.start()

    def seed_hop(step, act):
        for link, sign in ((0, -1), (1, 1)):
            if step < ZED // 2 - link:
                block = s_all.at[lax.rem(z + sign * step + ZED, ZED)]
                act(remote(block, block, seed_s.at[link, step], seed_r.at[link, step], links[link]))

    def start(copy):
        copy.start()

    def receive(copy):
        copy.wait_recv()

    def sent(copy):
        copy.wait_send()

    def pass_word():
        pl.semaphore_signal(word.at[0], inc=1, device_id=y_up, device_id_type=MESH)
        if ring > 2:
            pl.semaphore_signal(word.at[1], inc=1, device_id=y_down, device_id_type=MESH)

    def take_word():
        pl.semaphore_wait(word.at[0], 1)
        if ring > 2:
            pl.semaphore_wait(word.at[1], 1)

    n_chunks = 2
    chunk = width // 2 // n_chunks

    def width_part(i):
        return pl.ds(pl.multiple_of((c * n_chunks + i) * chunk, chunk), chunk)

    def hash_members():
        pick = lane == q * 8 + sub
        columns = [
            jnp.sum(
                jnp.where(pick, anchor_of(s_chip[0:1, :], s_chip[1:2, :] + 1, slot), 0), axis=1, keepdims=True
            )
            for slot in range(4)
        ]
        wide = lax.broadcasted_iota(jnp.int32, (8, chunk), 1)
        for i in range(n_chunks):
            first = (c * n_chunks + i) * chunk
            vbuf[0:8, i * chunk : (i + 1) * chunk] = stream(columns[0], wide + first)
            vbuf[8:16, i * chunk : (i + 1) * chunk] = stream(columns[2], wide + first)
        here = m * cols + c * half + lax.broadcasted_iota(jnp.int32, (8, half), 1)
        cbuf[0:8, :] = stream(columns[1], here) * SIGMA
        cbuf[8:16, :] = stream(columns[3], here) * SIGMA

    def project(i):
        own = lax.dot_general(
            xall[:, width_part(i)],
            vbuf[:, i * chunk : (i + 1) * chunk].astype(jnp.bfloat16),
            (((1,), (1,)), ((), ())),
            preferred_element_type=jnp.float32,
        )
        u_own[:, 0:16] = own if i == 0 else u_own[:, 0:16] + own

    seq = 2 * tokens // 8

    def rank_one():
        for i in range(8):
            r = slice(i * seq, (i + 1) * seq)
            for index in range(2):
                s = slice(index * half, (index + 1) * half)
                j = index * 8 + i
                along = u_own[r, j : j + 1] + u_sib[r, j : j + 1]
                acc[r, s] += along * cbuf[j : j + 1, :]

    def block_of(offset, other, core):
        zz = lax.rem(z + offset + ZED, ZED)
        return pop_of(zz, 1 - xl if other else xl, 1 - c if core else c)

    def multiply(*pieces):
        firsts = [block_of(*piece) for piece in pieces]
        ks = [pl.ds(pl.multiple_of(first * rows, rows), rows) for first in firsts]
        x = jnp.concatenate([xall[:, k] for k in ks], axis=1) if len(ks) > 1 else xall[:, ks[0]]
        w = jnp.concatenate([wbuf[first] for first in firsts], axis=0) if len(ks) > 1 else wbuf[firsts[0]]
        acc[...] += jnp.dot(x, w, preferred_element_type=jnp.float32)

    def multiply_chip(offset, other=None):
        zz = lax.rem(z + offset + ZED, ZED)
        if other is None:
            first, count = pop_of(zz, 0, 0), 4
        else:
            first, count = pop_of(zz, 1 - xl if other else xl, 0), 2
        depth = count * rows
        k = pl.ds(pl.multiple_of(first * rows, depth), depth)
        w = wbuf[pl.ds(first, count)].reshape(depth, cols)
        acc[...] += jnp.dot(xall[:, k], w, preferred_element_type=jnp.float32)

    give_along = remote(u_own, u_sib, one_s.at[4], one_r.at[4], sibling)
    acc[...] = jnp.zeros_like(acc)
    u_own[...] = jnp.zeros_like(u_own)
    pass_word()
    hash_members()
    arrive(0)
    take_word()
    give_chip.wait_recv()
    s_all[z] = s_chip[...] + s_side[...]
    seed_hop(0, start)
    pass_word()
    arrive(1)
    take_word()
    seed_hop(0, receive)
    seed_hop(1, start)
    pass_word()
    own_prompts.wait()
    arrive(2)
    take_word()
    seed_hop(1, receive)
    seed_hop(2, start)
    pass_word()
    give_prompts.wait_recv()
    project(0)
    multiply_chip(0)
    arrive(3)
    take_word()
    seed_hop(2, receive)
    seed_hop(3, start)
    project(1)
    give_along.start()
    multiply_chip(-1)
    arrive(4)
    seed_hop(3, receive)
    table = s_all[0]
    for i in range(1, ZED):
        table = table + s_all[i]
    seed_row = table[0:1, :]
    count_row = table[1:2, :]
    fit_row = (table[2:3, :].astype(jnp.float32) + 0.5) / members_all - 0.5
    left_gate = anchor_of(seed_row, count_row, 0)
    left_up = anchor_of(seed_row, count_row, 2)
    right_gate = anchor_of(seed_row, count_row, 1)
    right_up = anchor_of(seed_row, count_row, 3)
    scaling = RATE / (members_all * SIGMA)

    def hash_left(row, target, start):
        position = row + lax.broadcasted_iota(jnp.int32, (128, 128), 0)
        target[pl.ds(start, 128), 0:128] = (stream(left_gate, position) * fit_row).astype(jnp.bfloat16)
        target[pl.ds(start, 128), 128:256] = (stream(left_up, position) * fit_row).astype(jnp.bfloat16)

    def hash_width(first, count):
        def step(i, carry):
            hash_left(c * (width // 2) + i * 128, lbuf, pl.multiple_of(i * 128, 128))
            return carry

        lax.fori_loop(first, first + count, step, 0)

    def hash_right():
        def step(i, carry):
            start = pl.multiple_of(i * 128, 128)
            position = m * cols + start + lax.broadcasted_iota(jnp.int32, (128, 128), 0)
            rbuf[pl.ds(start, 128), 0:128] = stream(right_gate, position).astype(jnp.bfloat16)
            rbuf[pl.ds(start, 128), 128:256] = stream(right_up, position).astype(jnp.bfloat16)
            return carry

        lax.fori_loop(0, cols // 128, step, 0)

    def fresh_rows():
        hash_left(p * rows, lown, 0)
        load_gate.wait()
        load_up.wait()
        for index, out in enumerate((new_gate, new_up)):
            part = pl.ds(index * 128, 128)
            delta = lax.dot_general(
                lown[:, part], rbuf[:, part], (((1,), (1,)), ((), ())), preferred_element_type=jnp.float32
            )
            out[...] = (wown[index].astype(jnp.float32) + scaling * delta).astype(out.dtype)

    def low_rank(i):
        own = jnp.dot(xall[:, width_part(i)], lbuf[i * chunk : (i + 1) * chunk, :], preferred_element_type=jnp.float32)
        z_own[...] = own if i == 0 else z_own[...] + own

    def add_low_rank():
        for index in range(2):
            part = slice(index * 128, index * 128 + 128)
            acc[:, index * half : (index + 1) * half] += lax.dot_general(
                ((z_own[:, part] + z_sib[:, part]) * scaling).astype(jnp.bfloat16),
                rbuf[pl.ds(pl.multiple_of(c * half, half), half), part],
                (((1,), (1,)), ((), ())),
                preferred_element_type=jnp.float32,
            )

    give_low = remote(z_own, z_sib, one_s.at[6], one_r.at[6], sibling)
    n_hash = width // 2 // 128
    hash_width(0, n_hash)
    arrive(5)
    for i in range(n_chunks):
        low_rank(i)
    give_low.start()
    multiply_chip(1)
    arrive(6)
    hash_right()
    fresh_rows()
    give_along.wait_recv()
    rank_one()
    arrive(7)
    multiply_chip(2)
    multiply_chip(4, 0)
    give_low.wait_recv()
    add_low_rank()
    arrive(8)
    multiply_chip(-2)
    multiply_chip(-3, 0)
    multiply_chip(3, 0)
    multiply((-3, 1, 0), (3, 1, 1), (4, 1, 0))
    arrive(9)
    multiply((-3, 1, 1), (3, 1, 0), (4, 1, 1))

    load_head.wait()
    head_row = v_head[my_cols].astype(jnp.float32).reshape(1, half)
    parts = []
    for i in range(8):
        r = slice(i * seq, (i + 1) * seq)
        gate = acc[r, 0:half]
        value = gate / (1.0 + jnp.exp(-gate)) * acc[r, half:cols]
        parts.append(jnp.sum(value, axis=0, keepdims=True))
    summed = jnp.sum(jnp.concatenate(parts, axis=0) * head_row, axis=1, keepdims=True)
    r_own[...] = jnp.where(lane == q * 8 + sub, summed, 0.0)

    give_reward = remote(r_own, r_sib, one_s.at[7], one_r.at[7], sibling)
    give_reward.start()
    give_reward.wait_recv()
    r_part[...] = r_own[...] + r_sib[...]
    r_all[m] = r_part[...]

    def part_copy(i):
        return remote(r_part, r_all.at[m], red_s.at[0, i], red_r.at[0, i], mp_peer(i))

    for i in range(len(mp_pairs)):
        part_copy(i).start()
    for i in range(len(mp_pairs)):
        part_copy(i).wait_recv()
    t_part[...] = jnp.sum(r_all[...], axis=0)
    t_all[q] = t_part[...]

    def total_copy(i):
        return remote(t_part, t_all.at[q], red_s.at[1, i], red_r.at[1, i], chip_peer(i))

    for i in range(len(chip_pairs)):
        total_copy(i).start()
    for i in range(len(chip_pairs)):
        total_copy(i).wait_recv()
    rewards = jnp.sum(jnp.sum(t_all[...], axis=0), axis=0, keepdims=True) / seq
    mean = jnp.sum(rewards, axis=1, keepdims=True) / members_all
    spread = jnp.sum((rewards - mean) ** 2, axis=1, keepdims=True) / members_all
    result = (rewards - mean) / jnp.sqrt(spread + 1e-05)
    scores[...] = jnp.broadcast_to(result, scores.shape)

    give_gate.wait_send()
    give_up.wait_send()
    give_seeds.wait_send()
    give_prompts.wait_send()
    give_reward.wait_send()
    for link in range(3):
        for index in range(STEPS):
            ring_copy(link, index).wait_send()
    give_chip.wait_send()
    give_low.wait_send()
    give_along.wait_send()
    for step in range(ZED // 2):
        seed_hop(step, sent)
    for i in range(len(mp_pairs)):
        part_copy(i).wait_send()
    for i in range(len(chip_pairs)):
        total_copy(i).wait_send()


def finish(gate, up, all_scores, new_gate, new_up, scores):
    new_gate[...] = gate[...]
    new_up[...] = up[...]
    first = lax.axis_index("pop") * scores.shape[0]
    lane = lax.broadcasted_iota(jnp.int32, all_scores.shape, 1)
    sub = lax.broadcasted_iota(jnp.int32, all_scores.shape, 0)
    for i in range(scores.shape[0]):
        scores[i] = jnp.sum(jnp.where((lane == first + i) & (sub == 0), all_scores[...], 0.0))


def shards(mp_size, prompts, gate_weight, up_weight, reward_head, member_seeds, counters, member_ranks):
    members_here, seq, width = prompts.shape
    rows, cols = gate_weight.shape
    tokens = members_here * seq
    half = cols // 2
    hbm = pl.BlockSpec(memory_space=pltpu.HBM)
    vmem = pl.BlockSpec(memory_space=pltpu.VMEM)
    smem = pl.BlockSpec(memory_space=pltpu.SMEM)
    tile_f32 = pltpu.VMEM((8, 128), jnp.float32)
    tile_i32 = pltpu.VMEM((8, 128), jnp.int32)
    dma = pltpu.SemaphoreType.DMA
    results = pl.pallas_call(
        functools.partial(kernel, mp_size),
        out_shape=(
            pltpu.VMEM((rows, cols), jnp.bfloat16),
            pltpu.VMEM((rows, cols), jnp.bfloat16),
            pltpu.VMEM((8, 128), jnp.float32),
        ),
        in_specs=[hbm] * 7,
        out_specs=(vmem,) * 3,
        scratch_shapes=[
            pltpu.SMEM((members_here,), jnp.int32),
            pltpu.SMEM((members_here,), jnp.int32),
            pltpu.SMEM((members_here,), jnp.int32),
            pltpu.VMEM((cols,), jnp.bfloat16),
            pltpu.VMEM((2 * tokens, width), jnp.bfloat16),
            pltpu.VMEM((2 * GROUP, rows, cols), jnp.bfloat16),
            pltpu.VMEM((2 * tokens, cols), jnp.float32),
            pltpu.VMEM((2 * tokens, 256), jnp.float32),
            pltpu.VMEM((2 * tokens, 256), jnp.float32),
            pltpu.VMEM((2 * tokens, 128), jnp.float32),
            pltpu.VMEM((2 * tokens, 128), jnp.float32),
            pltpu.VMEM((width // 2, 256), jnp.bfloat16),
            pltpu.VMEM((rows, 256), jnp.bfloat16),
            pltpu.VMEM((cols, 256), jnp.bfloat16),
            pltpu.VMEM((16, width // 2), jnp.float32),
            pltpu.VMEM((16, half), jnp.float32),
            pltpu.VMEM((2, rows, cols), jnp.bfloat16),
            tile_i32,
            tile_i32,
            tile_i32,
            tile_i32,
            pltpu.VMEM((ZED, 8, 128), jnp.int32),
            tile_f32,
            tile_f32,
            tile_f32,
            pltpu.VMEM((mp_size, 8, 128), jnp.float32),
            tile_f32,
            pltpu.VMEM((GROUP, 8, 128), jnp.float32),
            dma((3, STEPS)),
            dma((3, STEPS)),
            dma((8,)),
            dma((8,)),
            dma((2, ZED // 2)),
            dma((2, ZED // 2)),
            dma((2, GROUP)),
            dma((2, GROUP)),
            dma((9,)),
            pltpu.SemaphoreType.REGULAR((2,)),
        ],
        compiler_params=pltpu.CompilerParams(
            collective_id=0, has_side_effects=True, vmem_limit_bytes=60 * 1024 * 1024
        ),
        name="generation",
    )(
        member_seeds,
        counters,
        member_ranks,
        prompts.reshape(tokens, width),
        gate_weight,
        up_weight,
        reward_head,
    )
    return pl.pallas_call(
        finish,
        out_shape=(
            jax.ShapeDtypeStruct((rows, cols), jnp.bfloat16),
            jax.ShapeDtypeStruct((rows, cols), jnp.bfloat16),
            jax.ShapeDtypeStruct((members_here,), jnp.float32),
        ),
        in_specs=[vmem] * 3,
        out_specs=(vmem, vmem, smem),
        compiler_params=pltpu.CompilerParams(vmem_limit_bytes=8 * 1024 * 1024),
        name="finish",
    )(*results)


def solution(mesh):
    in_specs = (
        P("pop", None, None),
        P("pop", "mp"),
        P("pop", "mp"),
        P("mp"),
        P("pop"),
        P("pop"),
        P("pop"),
    )
    out_specs = (P("pop", "mp"), P("pop", "mp"), P("pop"))
    body = functools.partial(shards, mesh.shape["mp"])
    return jax.shard_map(body, mesh=mesh, in_specs=in_specs, out_specs=out_specs, check_vma=False)
```

```python
import functools

import jax
import jax.numpy as jnp
from jax import lax
from jax.experimental import pallas as pl
from jax.experimental.pallas import tpu as pltpu
from jax.sharding import PartitionSpec as P

MESH = pl.DeviceIdType.MESH
SIGMA = 0.004
RATE = 0.0016
ROOT3 = 1.7320508075688772
ZED = 8
GROUP = 16

UP_LINK = [(0, 0, 0), (0, 0, 1), (-1, 0, 0), (0, 1, 1), (-2, 0, 0), (-1, 0, 1), (-3, 0, 0), (-1, 1, 1), (-2, 0, 1), (-2, 1, 1)]
DOWN_LINK = [(0, 0, 0), (0, 0, 1), (0, 1, 0), (1, 0, 1), (1, 0, 0), (2, 0, 1), (1, 1, 0), (3, 0, 1), (2, 0, 0), (2, 1, 0)]
SIDE_LINK = [(0, 0, 0), (0, 0, 1), (-1, 0, 0), (1, 0, 1), (-2, 0, 0), (2, 0, 1), (-3, 0, 0), (3, 0, 1), (-4, 0, 0), (4, 0, 1)]
SENDS = [UP_LINK, DOWN_LINK, SIDE_LINK]
ARRIVALS = [
    [(o - 1, w, h) for o, w, h in UP_LINK],
    [(o + 1, w, h) for o, w, h in DOWN_LINK],
    [(o, 1 - w, h) for o, w, h in SIDE_LINK],
]
STEPS = len(UP_LINK)


def same_piece(a, b):
    return (a[0] - b[0]) % ZED == 0 and a[1:] == b[1:]


def right_shift(v, amount):
    return lax.shift_right_logical(v, jnp.full_like(v, amount))


def mix(v):
    v = v ^ right_shift(v, 16)
    v = v * 2146121005
    v = v ^ right_shift(v, 15)
    v = v * -2073254261
    return v ^ right_shift(v, 16)


def anchor_of(seed, counter, slot):
    return mix(seed * 1103515245 + mix(counter * 668265263 + slot * 374761393))


def stream(anchor, position):
    h = mix(anchor + position * -1640531535)
    odd = (right_shift(h, 7) | 1) - 16777216
    return odd.astype(jnp.float32) * (ROOT3 / 16777216.0)


def kernel(
    mp_size, seeds, counters, ranks, prompts, gate_w, up_w, head,
    new_gate, new_up, scores,
    s_seeds, s_counters, s_ranks, v_head, xall, wbuf, acc, z_own, z_sib, u_own, u_sib, lbuf, lown, rbuf, vbuf, cbuf, wown,
    s_own, s_sib, s_chip, s_side, s_all, r_own, r_sib, r_part, r_all, t_part, t_all,
    ring_s, ring_r, one_s, one_r, seed_s, seed_r, red_s, red_r, local_sem, word,
):
    rows, cols = gate_w.shape
    half = cols // 2
    tokens, width = prompts.shape
    members_here = seeds.shape[0]
    p = lax.axis_index("pop")
    m = lax.axis_index("mp")
    z = p // 4
    xl = lax.rem(p // 2, 2)
    c = lax.rem(p, 2)
    q = p // 2
    members_all = 128

    def pop_of(zz, xx, cc):
        return (zz * 2 + xx) * 2 + cc

    sibling = (pop_of(z, xl, 1 - c), m)
    up = (pop_of(lax.rem(z + 1, ZED), xl, c), m)
    down = (pop_of(lax.rem(z + ZED - 1, ZED), xl, c), m)
    side = (pop_of(z, 1 - xl, c), m)
    links = [up, down, side]

    def by_distance(count, sides):
        pairs = [(o, w) for o in range(count) for w in range(sides) if o or w]
        return sorted(pairs, key=lambda pair: -min(pair[0], count - pair[0]))

    chip_pairs = by_distance(ZED, 2)

    def chip_peer(i):
        o, w = chip_pairs[i]
        return (pop_of(lax.rem(z + o, ZED), 1 - xl if w else xl, c), m)

    ring = min(mp_size, 8)
    y = lax.rem(m, ring)
    base = m - y
    y_up = (p, base + lax.rem(y + 1, ring))
    y_down = (p, base + lax.rem(y + ring - 1, ring))
    across = (p, lax.rem(m + ring, mp_size))

    mp_pairs = by_distance(ring, mp_size // ring)

    def mp_peer(i):
        o, w = mp_pairs[i]
        return (p, lax.rem((base + ring if w else base), mp_size) + lax.rem(y + o, ring))

    barrier = pltpu.get_barrier_semaphore()
    near = [sibling, up, down, side, y_up]
    if ring > 2:
        near.append(y_down)
    if mp_size > ring:
        near.append(across)
    for device in near:
        pl.semaphore_signal(barrier, inc=1, device_id=device, device_id_type=MESH)

    my_cols = pl.ds(pl.multiple_of(c * half, half), half)
    sib_cols = pl.ds(pl.multiple_of((1 - c) * half, half), half)
    own_rows = pl.ds(pl.multiple_of(c * tokens, tokens), tokens)
    keep_gate = pltpu.make_async_copy(gate_w.at[:, my_cols], wbuf.at[p, :, pl.ds(0, half)], local_sem.at[0])
    keep_up = pltpu.make_async_copy(up_w.at[:, my_cols], wbuf.at[p, :, pl.ds(half, half)], local_sem.at[1])
    keep_gate.start()
    keep_up.start()
    own_prompts = pltpu.make_async_copy(prompts, xall.at[own_rows], local_sem.at[2])
    own_prompts.start()
    load_gate = pltpu.make_async_copy(gate_w, wown.at[0], local_sem.at[3])
    load_up = pltpu.make_async_copy(up_w, wown.at[1], local_sem.at[4])
    load_gate.start()
    load_up.start()
    load_head = pltpu.make_async_copy(head, v_head, local_sem.at[5])
    load_head.start()
    ints = [(seeds, s_seeds), (counters, s_counters), (ranks, s_ranks)]
    load_ints = [pltpu.make_async_copy(a, b, local_sem.at[6 + i]) for i, (a, b) in enumerate(ints)]
    for load in load_ints:
        load.start()

    pl.semaphore_wait(barrier, len(near))

    def remote(src, dst, send, recv, device):
        return pltpu.make_async_remote_copy(
            src_ref=src, dst_ref=dst, send_sem=send, recv_sem=recv, device_id=device, device_id_type=MESH
        )

    give_gate = remote(gate_w.at[:, sib_cols], wbuf.at[p, :, pl.ds(0, half)], one_s.at[0], one_r.at[0], sibling)
    give_up = remote(up_w.at[:, sib_cols], wbuf.at[p, :, pl.ds(half, half)], one_s.at[1], one_r.at[1], sibling)
    give_seeds = remote(s_own, s_sib, one_s.at[2], one_r.at[2], sibling)
    give_prompts = remote(prompts, xall.at[own_rows], one_s.at[3], one_r.at[3], sibling)
    give_gate.start()
    give_up.start()

    def ring_copy(link, index):
        offset, other, core = SENDS[link][index]
        column = 1 - xl if other else xl
        where = pop_of(lax.rem(z + offset + 2 * ZED, ZED), column, 1 - c if core else c)
        piece = wbuf.at[where]
        return remote(piece, piece, ring_s.at[link, index], ring_r.at[link, index], links[link])

    def pass_on(piece):
        for link in range(3):
            for index, sent in enumerate(SENDS[link]):
                if same_piece(piece, sent):
                    ring_copy(link, index).start()

    def arrive(step):
        for link in range(3):
            ring_copy(link, step).wait_recv()
            pass_on(ARRIVALS[link][step])

    keep_gate.wait()
    keep_up.wait()
    for link in range(3):
        ring_copy(link, 0).start()
    give_gate.wait_recv()
    give_up.wait_recv()
    for link in range(3):
        ring_copy(link, 1).start()
    for load in load_ints:
        load.wait()
    lane = lax.broadcasted_iota(jnp.int32, (8, 128), 1)
    sub = lax.broadcasted_iota(jnp.int32, (8, 128), 0)
    block = jnp.zeros((8, 128), jnp.int32)
    for i in range(members_here):
        here = lane == p * members_here + i
        for row, values in enumerate((s_seeds, s_counters, s_ranks)):
            block = jnp.where(here & (sub == row), values[i], block)
    s_own[...] = block
    give_seeds.start()
    give_prompts.start()

    give_seeds.wait_recv()
    s_chip[...] = s_own[...] + s_sib[...]
    give_chip = remote(s_chip, s_side, one_s.at[5], one_r.at[5], side)
    give_chip.start()

    def seed_hop(step, act):
        for link, sign in ((0, -1), (1, 1)):
            if step < ZED // 2 - link:
                block = s_all.at[lax.rem(z + sign * step + ZED, ZED)]
                act(remote(block, block, seed_s.at[link, step], seed_r.at[link, step], links[link]))

    def start(copy):
        copy.start()

    def receive(copy):
        copy.wait_recv()

    def sent(copy):
        copy.wait_send()

    def pass_word():
        pl.semaphore_signal(word.at[0], inc=1, device_id=y_up, device_id_type=MESH)
        if ring > 2:
            pl.semaphore_signal(word.at[1], inc=1, device_id=y_down, device_id_type=MESH)

    def take_word():
        pl.semaphore_wait(word.at[0], 1)
        if ring > 2:
            pl.semaphore_wait(word.at[1], 1)

    n_chunks = 2
    chunk = width // 2 // n_chunks

    def width_part(i):
        return pl.ds(pl.multiple_of((c * n_chunks + i) * chunk, chunk), chunk)

    def hash_members():
        pick = lane == q * 8 + sub
        columns = [
            jnp.sum(
                jnp.where(pick, anchor_of(s_chip[0:1, :], s_chip[1:2, :] + 1, slot), 0), axis=1, keepdims=True
            )
            for slot in range(4)
        ]
        wide = lax.broadcasted_iota(jnp.int32, (8, chunk), 1)
        for i in range(n_chunks):
            first = (c * n_chunks + i) * chunk
            vbuf[0:8, i * chunk : (i + 1) * chunk] = stream(columns[0], wide + first)
            vbuf[8:16, i * chunk : (i + 1) * chunk] = stream(columns[2], wide + first)
        here = m * cols + c * half + lax.broadcasted_iota(jnp.int32, (8, half), 1)
        cbuf[0:8, :] = stream(columns[1], here) * SIGMA
        cbuf[8:16, :] = stream(columns[3], here) * SIGMA

    def project(i):
        own = lax.dot_general(
            xall[:, width_part(i)],
            vbuf[:, i * chunk : (i + 1) * chunk].astype(jnp.bfloat16),
            (((1,), (1,)), ((), ())),
            preferred_element_type=jnp.float32,
        )
        u_own[:, 0:16] = own if i == 0 else u_own[:, 0:16] + own

    seq = 2 * tokens // 8

    def rank_one():
        for i in range(8):
            r = slice(i * seq, (i + 1) * seq)
            for index in range(2):
                s = slice(index * half, (index + 1) * half)
                j = index * 8 + i
                along = u_own[r, j : j + 1] + u_sib[r, j : j + 1]
                acc[r, s] += along * cbuf[j : j + 1, :]

    def block_of(offset, other, core):
        zz = lax.rem(z + offset + ZED, ZED)
        return pop_of(zz, 1 - xl if other else xl, 1 - c if core else c)

    def multiply(*pieces):
        firsts = [block_of(*piece) for piece in pieces]
        ks = [pl.ds(pl.multiple_of(first * rows, rows), rows) for first in firsts]
        x = jnp.concatenate([xall[:, k] for k in ks], axis=1) if len(ks) > 1 else xall[:, ks[0]]
        w = jnp.concatenate([wbuf[first] for first in firsts], axis=0) if len(ks) > 1 else wbuf[firsts[0]]
        acc[...] += jnp.dot(x, w, preferred_element_type=jnp.float32)

    def whole(offset, other):
        return (offset, other, 0), (offset, other, 1)

    def multiply_chip(offset):
        first = pop_of(lax.rem(z + offset + ZED, ZED), 0, 0)
        depth = 4 * rows
        k = pl.ds(pl.multiple_of(first * rows, depth), depth)
        w = wbuf[pl.ds(first, 4)].reshape(depth, cols)
        acc[...] += jnp.dot(xall[:, k], w, preferred_element_type=jnp.float32)

    give_along = remote(u_own, u_sib, one_s.at[4], one_r.at[4], sibling)
    acc[...] = jnp.zeros_like(acc)
    u_own[...] = jnp.zeros_like(u_own)
    pass_word()
    hash_members()
    arrive(0)
    take_word()
    give_chip.wait_recv()
    s_all[z] = s_chip[...] + s_side[...]
    seed_hop(0, start)
    pass_word()
    arrive(1)
    take_word()
    seed_hop(0, receive)
    seed_hop(1, start)
    pass_word()
    own_prompts.wait()
    arrive(2)
    take_word()
    seed_hop(1, receive)
    seed_hop(2, start)
    pass_word()
    give_prompts.wait_recv()
    project(0)
    multiply_chip(0)
    arrive(3)
    take_word()
    seed_hop(2, receive)
    seed_hop(3, start)
    project(1)
    give_along.start()
    multiply_chip(-1)
    arrive(4)
    seed_hop(3, receive)
    table = s_all[0]
    for i in range(1, ZED):
        table = table + s_all[i]
    seed_row = table[0:1, :]
    count_row = table[1:2, :]
    fit_row = (table[2:3, :].astype(jnp.float32) + 0.5) / members_all - 0.5
    left_gate = anchor_of(seed_row, count_row, 0)
    left_up = anchor_of(seed_row, count_row, 2)
    right_gate = anchor_of(seed_row, count_row, 1)
    right_up = anchor_of(seed_row, count_row, 3)
    scaling = RATE / (members_all * SIGMA)

    def hash_left(row, target, start):
        position = row + lax.broadcasted_iota(jnp.int32, (128, 128), 0)
        target[pl.ds(start, 128), 0:128] = (stream(left_gate, position) * fit_row).astype(jnp.bfloat16)
        target[pl.ds(start, 128), 128:256] = (stream(left_up, position) * fit_row).astype(jnp.bfloat16)

    def hash_width(first, count):
        def step(i, carry):
            hash_left(c * (width // 2) + i * 128, lbuf, pl.multiple_of(i * 128, 128))
            return carry

        lax.fori_loop(first, first + count, step, 0)

    def hash_right():
        def step(i, carry):
            start = pl.multiple_of(i * 128, 128)
            position = m * cols + start + lax.broadcasted_iota(jnp.int32, (128, 128), 0)
            rbuf[pl.ds(start, 128), 0:128] = stream(right_gate, position).astype(jnp.bfloat16)
            rbuf[pl.ds(start, 128), 128:256] = stream(right_up, position).astype(jnp.bfloat16)
            return carry

        lax.fori_loop(0, cols // 128, step, 0)

    def fresh_rows():
        hash_left(p * rows, lown, 0)
        load_gate.wait()
        load_up.wait()
        for index, out in enumerate((new_gate, new_up)):
            part = pl.ds(index * 128, 128)
            delta = lax.dot_general(
                lown[:, part], rbuf[:, part], (((1,), (1,)), ((), ())), preferred_element_type=jnp.float32
            )
            out[...] = (wown[index].astype(jnp.float32) + scaling * delta).astype(out.dtype)

    def low_rank(i):
        own = jnp.dot(xall[:, width_part(i)], lbuf[i * chunk : (i + 1) * chunk, :], preferred_element_type=jnp.float32)
        z_own[...] = own if i == 0 else z_own[...] + own

    def add_low_rank():
        for index in range(2):
            part = slice(index * 128, index * 128 + 128)
            acc[:, index * half : (index + 1) * half] += lax.dot_general(
                ((z_own[:, part] + z_sib[:, part]) * scaling).astype(jnp.bfloat16),
                rbuf[pl.ds(pl.multiple_of(c * half, half), half), part],
                (((1,), (1,)), ((), ())),
                preferred_element_type=jnp.float32,
            )

    give_low = remote(z_own, z_sib, one_s.at[6], one_r.at[6], sibling)
    n_hash = width // 2 // 128
    hash_width(0, n_hash)
    arrive(5)
    for i in range(n_chunks):
        low_rank(i)
    give_low.start()
    multiply_chip(1)
    arrive(6)
    hash_right()
    fresh_rows()
    give_along.wait_recv()
    rank_one()
    arrive(7)
    multiply(*whole(2, 0), *whole(2, 1), *whole(4, 0), *whole(-2, 0))
    give_low.wait_recv()
    add_low_rank()
    arrive(8)
    multiply(*whole(-2, 1), (-3, 1, 0), (3, 1, 1), *whole(-3, 0), *whole(3, 0), (4, 1, 0))
    arrive(9)
    multiply((-3, 1, 1), (3, 1, 0), (4, 1, 1))

    load_head.wait()
    head_row = v_head[my_cols].astype(jnp.float32).reshape(1, half)
    parts = []
    for i in range(8):
        r = slice(i * seq, (i + 1) * seq)
        gate = acc[r, 0:half]
        value = gate / (1.0 + jnp.exp(-gate)) * acc[r, half:cols]
        parts.append(jnp.sum(value, axis=0, keepdims=True))
    summed = jnp.sum(jnp.concatenate(parts, axis=0) * head_row, axis=1, keepdims=True)
    r_own[...] = jnp.where(lane == q * 8 + sub, summed, 0.0)

    give_reward = remote(r_own, r_sib, one_s.at[7], one_r.at[7], sibling)
    give_reward.start()
    give_reward.wait_recv()
    r_part[...] = r_own[...] + r_sib[...]
    r_all[m] = r_part[...]

    def part_copy(i):
        return remote(r_part, r_all.at[m], red_s.at[0, i], red_r.at[0, i], mp_peer(i))

    for i in range(len(mp_pairs)):
        part_copy(i).start()
    for i in range(len(mp_pairs)):
        part_copy(i).wait_recv()
    t_part[...] = jnp.sum(r_all[...], axis=0)
    t_all[q] = t_part[...]

    def total_copy(i):
        return remote(t_part, t_all.at[q], red_s.at[1, i], red_r.at[1, i], chip_peer(i))

    for i in range(len(chip_pairs)):
        total_copy(i).start()
    for i in range(len(chip_pairs)):
        total_copy(i).wait_recv()
    rewards = jnp.sum(jnp.sum(t_all[...], axis=0), axis=0, keepdims=True) / seq
    mean = jnp.sum(rewards, axis=1, keepdims=True) / members_all
    spread = jnp.sum((rewards - mean) ** 2, axis=1, keepdims=True) / members_all
    result = (rewards - mean) / jnp.sqrt(spread + 1e-05)
    scores[...] = jnp.broadcast_to(result, scores.shape)

    give_gate.wait_send()
    give_up.wait_send()
    give_seeds.wait_send()
    give_prompts.wait_send()
    give_reward.wait_send()
    for link in range(3):
        for index in range(STEPS):
            ring_copy(link, index).wait_send()
    give_chip.wait_send()
    give_low.wait_send()
    give_along.wait_send()
    for step in range(ZED // 2):
        seed_hop(step, sent)
    for i in range(len(mp_pairs)):
        part_copy(i).wait_send()
    for i in range(len(chip_pairs)):
        total_copy(i).wait_send()


def finish(gate, up, all_scores, new_gate, new_up, scores):
    new_gate[...] = gate[...]
    new_up[...] = up[...]
    first = lax.axis_index("pop") * scores.shape[0]
    lane = lax.broadcasted_iota(jnp.int32, all_scores.shape, 1)
    sub = lax.broadcasted_iota(jnp.int32, all_scores.shape, 0)
    for i in range(scores.shape[0]):
        scores[i] = jnp.sum(jnp.where((lane == first + i) & (sub == 0), all_scores[...], 0.0))


def shards(mp_size, prompts, gate_weight, up_weight, reward_head, member_seeds, counters, member_ranks):
    members_here, seq, width = prompts.shape
    rows, cols = gate_weight.shape
    tokens = members_here * seq
    half = cols // 2
    hbm = pl.BlockSpec(memory_space=pltpu.HBM)
    vmem = pl.BlockSpec(memory_space=pltpu.VMEM)
    smem = pl.BlockSpec(memory_space=pltpu.SMEM)
    tile_f32 = pltpu.VMEM((8, 128), jnp.float32)
    tile_i32 = pltpu.VMEM((8, 128), jnp.int32)
    dma = pltpu.SemaphoreType.DMA
    results = pl.pallas_call(
        functools.partial(kernel, mp_size),
        out_shape=(
            pltpu.VMEM((rows, cols), jnp.bfloat16),
            pltpu.VMEM((rows, cols), jnp.bfloat16),
            pltpu.VMEM((8, 128), jnp.float32),
        ),
        in_specs=[hbm] * 7,
        out_specs=(vmem,) * 3,
        scratch_shapes=[
            pltpu.SMEM((members_here,), jnp.int32),
            pltpu.SMEM((members_here,), jnp.int32),
            pltpu.SMEM((members_here,), jnp.int32),
            pltpu.VMEM((cols,), jnp.bfloat16),
            pltpu.VMEM((2 * tokens, width), jnp.bfloat16),
            pltpu.VMEM((2 * GROUP, rows, cols), jnp.bfloat16),
            pltpu.VMEM((2 * tokens, cols), jnp.float32),
            pltpu.VMEM((2 * tokens, 256), jnp.float32),
            pltpu.VMEM((2 * tokens, 256), jnp.float32),
            pltpu.VMEM((2 * tokens, 128), jnp.float32),
            pltpu.VMEM((2 * tokens, 128), jnp.float32),
            pltpu.VMEM((width // 2, 256), jnp.bfloat16),
            pltpu.VMEM((rows, 256), jnp.bfloat16),
            pltpu.VMEM((cols, 256), jnp.bfloat16),
            pltpu.VMEM((16, width // 2), jnp.float32),
            pltpu.VMEM((16, half), jnp.float32),
            pltpu.VMEM((2, rows, cols), jnp.bfloat16),
            tile_i32,
            tile_i32,
            tile_i32,
            tile_i32,
            pltpu.VMEM((ZED, 8, 128), jnp.int32),
            tile_f32,
            tile_f32,
            tile_f32,
            pltpu.VMEM((mp_size, 8, 128), jnp.float32),
            tile_f32,
            pltpu.VMEM((GROUP, 8, 128), jnp.float32),
            dma((3, STEPS)),
            dma((3, STEPS)),
            dma((8,)),
            dma((8,)),
            dma((2, ZED // 2)),
            dma((2, ZED // 2)),
            dma((2, GROUP)),
            dma((2, GROUP)),
            dma((9,)),
            pltpu.SemaphoreType.REGULAR((2,)),
        ],
        compiler_params=pltpu.CompilerParams(
            collective_id=0, has_side_effects=True, vmem_limit_bytes=60 * 1024 * 1024
        ),
        name="generation",
    )(
        member_seeds,
        counters,
        member_ranks,
        prompts.reshape(tokens, width),
        gate_weight,
        up_weight,
        reward_head,
    )
    return pl.pallas_call(
        finish,
        out_shape=(
            jax.ShapeDtypeStruct((rows, cols), jnp.bfloat16),
            jax.ShapeDtypeStruct((rows, cols), jnp.bfloat16),
            jax.ShapeDtypeStruct((members_here,), jnp.float32),
        ),
        in_specs=[vmem] * 3,
        out_specs=(vmem, vmem, smem),
        compiler_params=pltpu.CompilerParams(vmem_limit_bytes=8 * 1024 * 1024),
        name="finish",
    )(*results)


def solution(mesh):
    in_specs = (
        P("pop", None, None),
        P("pop", "mp"),
        P("pop", "mp"),
        P("mp"),
        P("pop"),
        P("pop"),
        P("pop"),
    )
    out_specs = (P("pop", "mp"), P("pop", "mp"), P("pop"))
    body = functools.partial(shards, mesh.shape["mp"])
    return jax.shard_map(body, mesh=mesh, in_specs=in_specs, out_specs=out_specs, check_vma=False)
```
